256 devices in a mesh: dp: 2 (over core), ctx: 16 (over z, x_hi), tp: 8 (over y, x_lo).
Axes of the slice: x: 4 (x_hi: 2, x_lo: 2; x = x_hi * 2 + x_lo), y: 4, z: 8, core: 2. Of those that a mesh axis runs over, the one named last changes fastest.
Arguments:
- queries: bfloat16 [2, 4096, 2048], P('dp', 'ctx', 'tp'), may hold values from -32 to 32
- key_heads: bfloat16 [2, 4096, 2048], P('dp', 'ctx', 'tp'), may hold values from -32 to 32
- value_heads: bfloat16 [2, 4096, 2048], P('dp', 'ctx', 'tp'), may hold values from -6 to 6
- grad_output: bfloat16 [2, 4096, 4096], P('dp', 'ctx', 'tp'), may hold values from -6 to 6
- out_weight: bfloat16 [2048, 4096], P('tp'), may hold values from -0.375 to 0.375
- block_pattern: int32 [16, 3], replicated, may hold values from 0 to 15, all different within a row; in each aligned block of 16 rows (0 to 15, 16 to 31, ...) at most 6 rows name the same one
- global_offsets: int32 [16, 8], replicated, may hold values from 0 to 255, as said below
Outputs:
- grad_queries: bfloat16 [2, 4096, 2048], P('dp', 'ctx', 'tp')
- grad_keys: bfloat16 [2, 4096, 2048], P('dp', 'ctx', 'tp')
- grad_values: bfloat16 [2, 4096, 2048], P('dp', 'ctx', 'tp')
- grad_weight: bfloat16 [2048, 4096], P('tp', ('dp', 'ctx'))
The draws below stay inside these ranges and needn't reach their ends.
Inputs may be any that keep to these rules, and one draw needn't show every extreme that they name: `block_pattern`: each row names 3 different blocks; no block is named by more than 6 rows in all, and one block is named by exactly 6 rows. A row may name its own block or a neighbour. `global_offsets`: row b holds the positions within block b of its 8 global tokens, all different.
All inputs are finite; a program needn't handle non-finite values.
Results may differ from the reference program's by a relative error of at most 0.017.
Values may be sent and summed in bfloat16 or wider, within the bound.
A program may use at most 64 MiB of HBM per device.

```python
import math
import jax
import jax.numpy as jnp
import numpy as np
from jax import lax

D = 4096
HD = 128
BLK = 256
RAND = 3
GB = 8
MOST = 6
NBLK = 16
SEQ = 4096
BATCH = 2
FEATS = 2048


def offset_table(key):
    table_key = jax.random.fold_in(key, 7)
    priority = jax.random.randint(table_key, (NBLK, BLK), 0, 1 << 20, dtype=jnp.int32) * BLK
    priority = priority + jnp.arange(BLK, dtype=jnp.int32)[None, :]
    return jnp.argsort(priority, axis=1)[:, :GB + 5].astype(jnp.int32)


def drawn_floats(key, stream_id):
    full_shape = (BATCH, SEQ, FEATS)
    return jnp.clip(jax.random.normal(jax.random.fold_in(key, stream_id), full_shape, dtype=jnp.float32), -4.0, 4.0)


def draw_queries(key, part):
    values = drawn_floats(key, 21)
    return values.astype(jnp.bfloat16)


def draw_key_heads(key, part):
    key_ramp = 0.6 + 1.2 * jnp.arange(SEQ, dtype=jnp.float32) / SEQ
    values = drawn_floats(key, 31) * key_ramp[None, :, None]
    return values.astype(jnp.bfloat16)


def draw_global_offsets(key, part):
    return offset_table(key)[:, :GB]


def with_spikes(result, stream_key, source, target, shards_of, factor):
    def block_of(axis_at):
        return (jnp.arange(result.shape[axis_at]) // (result.shape[axis_at] // shards_of)).reshape((-1,) + (1,) * (result.ndim - 1 - axis_at))

    first = jax.random.permutation(stream_key, shards_of)[block_of(target)]
    other_side = (block_of(target) + shards_of // 2) % shards_of
    return jnp.where((block_of(source) == first) | (block_of(source) == other_side), factor * result, result)


def steps_of(stream_key, extent, split, least, high):
    def one(position, shards_of):
        draws = jax.random.uniform(jax.random.fold_in(jax.random.fold_in(stream_key, 6), position), (shards_of,), jnp.float32, least / len(split), high / len(split))
        return jnp.repeat(jnp.exp(draws), extent[position] // shards_of).reshape((-1,) + (1,) * (len(extent) - position - 1))

    gain = one(*split[0])
    for cut in split[1:]:
        gain = gain * one(*cut)
    return gain


def shared_out(key, own, number, rows, number_of, top, limit, lean):
    order = jax.random.permutation(key, number_of)
    heavy_load, usual = load_shares(number_of, rows * top, limit, lean, True), load_shares(number_of, rows * top, limit, lean, False)
    places = jnp.arange(number_of)

    def named(lengths, turn):
        used = int((lengths > 0).sum())
        fixed = max(1, used // 4)
        moved = fixed + (places - fixed + turn * (used - fixed)) % max(1, number_of - fixed)
        return jnp.zeros((number_of,), jnp.int32).at[order[jnp.where(places < fixed, places, moved)]].set(jnp.asarray(lengths, jnp.int32))

    lengths = jnp.where(number % 4 == 0, named(heavy_load, number // 4), named(usual, number - number // 4 - 1))
    mixed = jax.random.permutation(jax.random.fold_in(own, 3), number_of)
    giver, taker = mixed[0:number_of // 2 * 2:2], mixed[1:number_of // 2 * 2:2]
    slack = jnp.minimum(lengths[giver] - 1, limit - lengths[taker]) // 2
    slack = jnp.where((giver == order[0]) | (taker == order[0]) | (lengths[taker] == 0), 0, jnp.maximum(slack, 0))
    moved = jax.random.randint(jax.random.fold_in(own, 4), (number_of // 2,), 0, 1 << 20) % (slack + 1)
    lengths = lengths.at[giver].add(-moved).at[taker].add(moved)
    labels = jnp.searchsorted(jnp.cumsum(lengths), jnp.arange(rows * top), side="right").astype(jnp.int32)
    table = labels.reshape(top, rows).T
    table = table[jax.random.permutation(jax.random.fold_in(own, 1), rows)]
    turn = jax.random.randint(jax.random.fold_in(own, 2), (rows, 1), 0, top)
    return jnp.take_along_axis(table, (jnp.arange(top)[None, :] + turn) % top, axis=1)


def load_shares(amount, total, most, skew, full):
    portions = [(1 << 20) // math.isqrt(standing ** skew) + 1 for standing in range(1, amount + 1)]
    largest = most if full else min(most, max(-(-total // amount), total * portions[0] // sum(portions)))
    least = 1 if total - largest >= amount - 1 else 0
    holding, rest = [largest] + [least] * (amount - 1), total - largest - least * (amount - 1)
    while rest > 0:
        movable = [i for i in range(1, amount) if holding[i] < largest] or [i for i in range(1, amount) if holding[i] < most]
        whole, remaining = sum([portions[i] for i in movable]), rest
        for i in movable:
            extra = min(most - holding[i], max(1, remaining * portions[i] // whole), rest)
            holding[i] = holding[i] + extra
            rest = rest - extra
    return np.array(holding)


def scatter_about(rng, shape, spread, reach, cuts=(), held_as=jnp.bfloat16):
    loudness = steps_of(rng, shape, cuts, -0.22, 0.18) if cuts else 1.0
    values = jax.random.normal(rng, shape, jnp.float32) * spread * loudness
    return jnp.minimum(jnp.maximum(values, -reach), reach).astype(held_as)


def gaussian_with(rng, extent, width, limit, cuts, heavy, kind=jnp.bfloat16):
    entries = width * jax.random.normal(rng, extent, jnp.float32)
    if cuts:
        entries = entries * steps_of(rng, extent, cuts, -0.22, 0.18)
    return jnp.clip(with_spikes(entries, jax.random.fold_in(rng, 3), *heavy), -limit, limit).astype(kind)


def setup_inputs(seed: int = 0) -> dict:
    keys = jax.random.split(jax.random.key(seed), 8)
    queries = draw_queries(jax.random.fold_in(keys[7], 71), 0)
    key_heads = draw_key_heads(jax.random.fold_in(keys[7], 71), 0)
    value_heads = scatter_about(keys[2], (BATCH, SEQ, FEATS), 1.0, 6.0, ((0, 2), (1, 16), (2, 8)))
    grad_output = gaussian_with(keys[3], (BATCH, SEQ, D), 1.0, 6.0, ((0, 2), (1, 16), (2, 8)), (1, 2, 16, 2.0))
    out_weight = scatter_about(keys[4], (FEATS, D), (D // 16) ** -0.5, 0.375, ((0, 8),))
    block_pattern_keys = jax.random.split(jax.random.fold_in(keys[5], 1), NBLK // NBLK)
    block_pattern_turns = jax.random.permutation(jax.random.fold_in(keys[5], 3), NBLK // NBLK)
    block_pattern = jax.vmap(lambda own, number: shared_out(jax.random.fold_in(keys[5], 2), own, number, NBLK, NBLK, RAND, MOST, 2))(block_pattern_keys, block_pattern_turns).reshape((NBLK, RAND))
    global_offsets = draw_global_offsets(jax.random.fold_in(keys[7], 71), 0)
    return {"queries": queries, "key_heads": key_heads, "value_heads": value_heads, "grad_output": grad_output, "out_weight": out_weight, "block_pattern": block_pattern, "global_offsets": global_offsets}


def rounded(values):
    return lax.optimization_barrier(values.astype(jnp.bfloat16)).astype(jnp.float32)


def softmax_last(scores):
    row_max = jnp.max(scores, axis=-1, keepdims=True)
    weights_f = jnp.exp(scores - row_max)
    row_total = jnp.sum(weights_f, axis=-1, keepdims=True)
    return weights_f / row_total


def document(query_doc, key_doc, value_doc, grad_doc, out_weight, block_pattern, global_offsets):
    token_count, feature_count = query_doc.shape
    block_count = block_pattern.shape[0]
    block_size = token_count // block_count
    head_count = feature_count // HD
    score_scale = HD ** -0.5
    grad_heads = jnp.dot(grad_doc, out_weight.T, preferred_element_type=jnp.float32).astype(jnp.bfloat16)
    query_all = query_doc.reshape(token_count, head_count, HD).astype(jnp.float32)
    key_all = key_doc.reshape(token_count, head_count, HD).astype(jnp.float32)
    value_all = value_doc.reshape(token_count, head_count, HD).astype(jnp.float32)
    grad_all = grad_heads.reshape(token_count, head_count, HD).astype(jnp.float32)
    positions = jnp.arange(block_size, dtype=jnp.int32)
    glob_flags = jnp.any(global_offsets[:, :, None] == positions[None, None, :], axis=1)
    glob_positions = (jnp.arange(block_count, dtype=jnp.int32)[:, None] * block_size + global_offsets).reshape(-1)

    def one_block(carry, own_block):
        row_keep = jnp.logical_not(glob_flags[own_block])
        own_offsets = global_offsets[own_block]
        neighbours = own_block + jnp.arange(-1, 2, dtype=jnp.int32)
        chosen = block_pattern[own_block]
        slot_ok = jnp.concatenate([(neighbours >= 0) & (neighbours < block_count), jnp.abs(chosen - own_block) > 1])
        slot_clip = jnp.clip(jnp.concatenate([neighbours, chosen]), 0, block_count - 1).astype(jnp.int32)
        slot_rows = (slot_clip[:, None] * block_size + positions[None, :]).reshape(-1)
        key_index = jnp.concatenate([slot_rows, glob_positions]).astype(jnp.int32)
        slot_valid = (slot_ok[:, None] & jnp.logical_not(glob_flags[slot_clip])).reshape(-1)
        key_valid = jnp.concatenate([slot_valid, glob_positions >= 0])
        block_start = (own_block * block_size).astype(jnp.int32)
        query_block = lax.dynamic_slice_in_dim(query_all, block_start, block_size, 0)
        grad_block = lax.dynamic_slice_in_dim(grad_all, block_start, block_size, 0)
        key_pick = jnp.take(key_all, key_index, axis=0)
        value_pick = jnp.take(value_all, key_index, axis=0)
        scores = score_scale * jnp.einsum('qhd,khd->hqk', query_block, key_pick)
        scores = jnp.where(key_valid[None, None, :], scores, -jnp.inf)
        attn_probs = jnp.where(row_keep[None, :, None], softmax_last(scores), 0.0)
        probs_low = rounded(attn_probs)
        glob_query = jnp.take(query_block, own_offsets, axis=0)
        glob_grad = jnp.take(grad_block, own_offsets, axis=0)
        glob_probs = softmax_last(score_scale * jnp.einsum('ghd,khd->hgk', glob_query, key_all))
        glob_low = rounded(glob_probs)
        attention = jnp.einsum('hqk,khd->qhd', probs_low, value_pick)
        attention = attention.at[own_offsets].set(jnp.einsum('hgk,khd->ghd', glob_low, value_all))
        attention = attention.astype(jnp.bfloat16)
        row_dot = jnp.sum(grad_block * attention.astype(jnp.float32), axis=2)
        glob_dot = jnp.take(row_dot, own_offsets, axis=0)
        grad_probs = jnp.einsum('qhd,khd->hqk', grad_block, value_pick)
        dscore_low = rounded(attn_probs * (grad_probs - row_dot.T[:, :, None]))
        glob_dscore = rounded(glob_probs * (jnp.einsum('ghd,khd->hgk', glob_grad, value_all) - glob_dot.T[:, :, None]))
        grad_query = jnp.einsum('hqk,khd->qhd', dscore_low, key_pick)
        grad_query = grad_query.at[own_offsets].set(jnp.einsum('hgk,khd->ghd', glob_dscore, key_all))
        grad_query = (score_scale * grad_query).astype(jnp.bfloat16)
        glob_term = jnp.stack([score_scale * jnp.einsum('hgk,ghd->khd', glob_dscore, glob_query),
                               jnp.einsum('hgk,ghd->khd', glob_low, glob_grad)], axis=1)
        pick_term = jnp.stack([score_scale * jnp.einsum('hqk,qhd->khd', dscore_low, query_block),
                               jnp.einsum('hqk,qhd->khd', probs_low, grad_block)], axis=1)
        key_term = glob_term.at[key_index].add(pick_term)
        return carry + rounded(key_term), (grad_query, attention)

    zeros = jnp.zeros((token_count, 2, head_count, HD), jnp.float32)
    summed, (grad_query, attention) = lax.scan(one_block, zeros, jnp.arange(block_count, dtype=jnp.int32))
    grad_queries = grad_query.reshape(token_count, feature_count)
    grad_keys = summed[:, 0].reshape(token_count, feature_count).astype(jnp.bfloat16)
    grad_values = summed[:, 1].reshape(token_count, feature_count).astype(jnp.bfloat16)
    weight_terms = jnp.dot(attention.reshape(token_count, feature_count).T, grad_doc, preferred_element_type=jnp.float32)
    return grad_queries, grad_keys, grad_values, weight_terms


def reference(queries, key_heads, value_heads, grad_output, out_weight, block_pattern, global_offsets):
    results = [document(queries[doc_index], key_heads[doc_index], value_heads[doc_index], grad_output[doc_index],
                        out_weight, block_pattern, global_offsets) for doc_index in range(queries.shape[0])]
    grad_queries = jnp.stack([entry[0] for entry in results])
    grad_keys = jnp.stack([entry[1] for entry in results])
    grad_values = jnp.stack([entry[2] for entry in results])
    weight_sum = results[0][3]
    for entry in results[1:]:
        weight_sum = weight_sum + entry[3]
    return grad_queries, grad_keys, grad_values, weight_sum.astype(jnp.bfloat16)
```

```python
import functools

import jax
import jax.numpy as jnp
from jax import lax
from jax.experimental import pallas as pl
from jax.experimental.pallas import tpu as pltpu
from jax.sharding import PartitionSpec as P

HD = 128
LOWEST = -1e30
SCALE = HD ** (-0.5)
LOG2E = 1.4426950408889634
MESH = pl.DeviceIdType.MESH
F32 = jnp.float32
BF16 = jnp.bfloat16


def nt(a, b):
    return lax.dot_general(a, b, (((1,), (1,)), ((), ())), preferred_element_type=F32)


def tn(a, b):
    return lax.dot_general(a, b, (((0,), (0,)), ((), ())), preferred_element_type=F32)


def nn(a, b):
    return jnp.dot(a, b, preferred_element_type=F32)


def any_of(flags):
    return functools.reduce(jnp.logical_or, flags)


class Sems:
    def __init__(self):
        self.index = {}

    def __getitem__(self, name):
        return self.index.setdefault(name, len(self.index))


N_SEM = 80


def kernel(
    nz,
    ny,
    pat,
    offs,
    q_hbm,
    k_hbm,
    v_hbm,
    g_hbm,
    w_hbm,
    dq_hbm,
    dk_hbm,
    dv_hbm,
    gw_hbm,
    kv,
    q2,
    do2,
    gb,
    wv,
    gh,
    ghb,
    kb,
    qb,
    sb,
    mx,
    lr,
    stat,
    ot,
    ob,
    att,
    pb,
    db,
    own,
    snd,
    rp,
    rm,
    dqt,
    dqb,
    fin,
    gws,
    gwr,
    gwo,
    gsn,
    gp,
    gm,
    gfin,
    gxr,
    gout,
    ss,
    rs,
    ls,
):
    T = q_hbm.shape[1]
    Q2 = 2 * T
    nctx, ntp = 2 * nz, 2 * ny
    DC = g_hbm.shape[2]
    F = w_hbm.shape[0]
    CW = gw_hbm.shape[1]
    GB = offs.shape[1]
    up, dn = nz // 2, max(nz // 2 - 1, 0)
    yup, ydn = ny // 2, max(ny // 2 - 1, 0)
    lanes = [slice(i * 128, (i + 1) * 128) for i in range(Q2 // 128)]

    d = lax.axis_index("dp")
    c = lax.axis_index("ctx")
    t = lax.axis_index("tp")
    z, h = lax.div(c, 2), lax.rem(c, 2)
    y, xl = lax.div(t, 2), lax.rem(t, 2)
    o = 1 - h

    def at_z(step):
        return lax.rem(z + (step + nz), nz)

    def at_y(step):
        return lax.rem(y + (step + ny), ny)

    def zdev(step):
        return (d, at_z(step) * 2 + h, t)

    def ydev(step):
        return (d, c, at_y(step) * 2 + xl)

    partner = (d, 2 * z + o, t)
    xdev = (d, c, 2 * y + 1 - xl)
    core = (1 - d, c, t)
    hcols = pl.ds(pl.multiple_of(h * HD, HD), HD)
    ocols = pl.ds(pl.multiple_of(o * HD, HD), HD)
    hrows = pl.ds(pl.multiple_of(h * T, T), T)
    orows = pl.ds(pl.multiple_of(o * T, T), T)

    sem = Sems()
    sent = []

    def send(name, src, dst, dev):
        i = sem[name]
        cp = pltpu.make_async_remote_copy(
            src_ref=src, dst_ref=dst, send_sem=ss.at[i], recv_sem=rs.at[i],
            device_id=dev, device_id_type=MESH,
        )
        cp.start()
        sent.append(cp)

    def arrive(name, dst):
        i = sem[name]
        pltpu.make_async_remote_copy(
            src_ref=dst, dst_ref=dst, send_sem=ss.at[i], recv_sem=rs.at[i],
            device_id=partner, device_id_type=MESH,
        ).wait_recv()

    def local(i, src, dst):
        cp = pltpu.make_async_copy(src, dst, ls.at[i])
        cp.start()
        return cp

    load_k = local(0, k_hbm.at[0, :, hcols], kv.at[c, 0])
    load_v = local(1, v_hbm.at[0, :, hcols], kv.at[c, 1])
    load_q = local(2, q_hbm.at[0, :, hcols], q2.at[hrows])
    load_g = local(3, g_hbm.at[0], gb.at[t])
    load_w = local(4, w_hbm, wv)

    near = [partner, xdev, core]
    if nz > 1:
        near += [zdev(1), zdev(-1)]
    if ny > 1:
        near += [ydev(1), ydev(-1)]
    barrier = pltpu.get_barrier_semaphore()
    for dev in near:
        pl.semaphore_signal(barrier, inc=1, device_id=dev, device_id_type=MESH)
    pl.semaphore_wait(barrier, len(near))

    hops = {("a", 1): up, ("a", -1): dn, ("b", 1): dn, ("b", -1): up}

    def z_block(chain, step):
        return 2 * at_z(step) + (h if chain == "a" else o)

    def z_send(chain, way, hop):
        if hop < hops[chain, way]:
            block = kv.at[z_block(chain, -way * hop)]
            send(("kv", chain, way, hop + 1), block, block, zdev(way))

    ghops = {("a", 1): yup, ("a", -1): ydn, ("b", 1): ydn, ("b", -1): yup}

    def y_piece(chain, step):
        return 2 * at_y(step) + (xl if chain == "a" else 1 - xl)

    def y_send(chain, way, hop):
        if hop < ghops[chain, way]:
            piece = gb.at[y_piece(chain, -way * hop)]
            src = g_hbm.at[0] if chain == "a" and hop == 0 else piece
            send(("g", chain, way, hop + 1), src, piece, ydev(way))

    send("gx", g_hbm.at[0], gb.at[t], xdev)
    y_send("a", 1, 0)
    y_send("a", -1, 0)
    load_k.wait()
    load_v.wait()
    z_send("a", 1, 0)
    z_send("a", -1, 0)
    send("k", k_hbm.at[0, :, ocols], kv.at[c, 0], partner)
    send("v", v_hbm.at[0, :, ocols], kv.at[c, 1], partner)
    send("q", q_hbm.at[0, :, ocols], q2.at[hrows], partner)

    lane = lax.broadcasted_iota(jnp.int32, (1, Q2), 1)
    is_first = lane < T
    pos = jnp.where(is_first, lane, lane - T)
    b0 = 2 * z
    bvec = jnp.where(is_first, b0, b0 + 1)

    def both(ref, k):
        return jnp.where(is_first, ref[b0, k], ref[b0 + 1, k])

    row_global = any_of([pos == both(offs, g) for g in range(GB)])
    picks = [both(pat, r) for r in range(pat.shape[1])]
    for cc in range(nctx):
        seen = any_of([row_global, jnp.abs(bvec - cc) <= 1] + [pick == cc for pick in picks])
        qb[cc] = jnp.where(seen, 0.0, LOWEST)

    def key_bias(cc, carry):
        row = lax.broadcasted_iota(jnp.int32, (T, 128), 0)
        kb[cc] = jnp.where(any_of([row == offs[cc, g] for g in range(GB)]), 0.0, LOWEST)
        return carry

    lax.fori_loop(0, nctx, key_bias, 0)
    mx[...] = jnp.full_like(mx, LOWEST)
    gh[...] = jnp.zeros_like(gh)

    def score(cc):
        s = nt(kv[cc, 0], q2[...])
        bias = kb[cc]
        row_bias = qb[cc]
        for sl in lanes:
            part = s[:, sl] + jnp.maximum(bias, row_bias[:, sl])
            sb[cc, :, sl] = part
            mx[:, sl] = jnp.maximum(mx[:, sl], jnp.max(part.reshape(T // 8, 8, 128), axis=0))

    def project(tt):
        cols = pl.ds(pl.multiple_of(tt * DC, DC), DC)
        gh[...] += nt(gb[tt], wv[:, cols])

    ready = {"q": False, "blocks": []}

    def scores_of(cc):
        if ready["q"]:
            score(cc)
        else:
            ready["blocks"].append(cc)

    def on_own():
        load_g.wait()
        load_w.wait()
        project(t)
        scores_of(z_block("a", 0))

    def on_q():
        load_q.wait()
        arrive("q", q2.at[orows])
        ready["q"] = True
        for cc in ready["blocks"]:
            score(cc)

    def on_pair():
        pair = z_block("b", 0)
        arrive("k", kv.at[pair, 0])
        arrive("v", kv.at[pair, 1])
        z_send("b", 1, 0)
        z_send("b", -1, 0)
        scores_of(pair)

    def on_gx():
        piece = y_piece("b", 0)
        arrive("gx", gb.at[piece])
        y_send("b", 1, 0)
        y_send("b", -1, 0)
        project(piece)

    def on_kv(chain, way, hop):
        block = z_block(chain, -way * hop)
        arrive(("kv", chain, way, hop), kv.at[block])
        z_send(chain, way, hop)
        scores_of(block)

    def on_g(chain, way, hop):
        piece = y_piece(chain, -way * hop)
        arrive(("g", chain, way, hop), gb.at[piece])
        y_send(chain, way, hop)
        project(piece)

    events = [(0.0, on_own), (7.0, on_gx), (12.5, on_pair), (15.0, on_q)]
    for (chain, way), count in hops.items():
        for hop in range(1, count + 1):
            when = (0.0 if chain == "a" else 12.6) + 4.5 * hop
            events.append((when, functools.partial(on_kv, chain, way, hop)))
    for (chain, way), count in ghops.items():
        for hop in range(1, count + 1):
            when = (0.0 if chain == "a" else 7.1) + 7.2 * hop
            events.append((when, functools.partial(on_g, chain, way, hop)))
    for _, event in sorted(events, key=lambda pair: pair[0]):
        event()

    ghb[0] = gh[:, :HD].astype(BF16)
    ghb[1] = gh[:, HD:].astype(BF16)
    send("do", ghb.at[o], do2.at[hrows], partner)
    do2[hrows, :] = ghb[h]

    stat[0] = jnp.max(mx[...], axis=0, keepdims=True)
    lr[...] = jnp.zeros_like(lr)
    ot[...] = jnp.zeros_like(ot)

    def weigh(cc, carry):
        for sl in lanes:
            e = jnp.exp2((sb[cc, :, sl] - stat[0, :, sl]) * (SCALE * LOG2E))
            sb[cc, :, sl] = e
            lr[:, sl] += jnp.sum(e.reshape(T // 8, 8, 128), axis=0)
            pb[:, sl] = e.astype(BF16)
        ot[...] += tn(kv[cc, 1], pb[...])
        return carry

    lax.fori_loop(0, nctx, weigh, 0)
    inverse = 1.0 / jnp.sum(lr[...], axis=0, keepdims=True)
    stat[1] = inverse
    low = (ot[...] * inverse).astype(BF16)
    ob[...] = low
    send("att", ob.at[:, orows], att.at[h], partner)
    att[h] = ob[:, hrows]
    arrive("do", do2.at[orows])
    do_t = jnp.transpose(do2[...].astype(F32))
    stat[2] = jnp.sum(do_t * low.astype(F32), axis=0, keepdims=True)
    dqt[...] = jnp.zeros_like(dqt)

    def gradients(zz):
        def one(x, carry):
            cc = 2 * zz + x
            dp = nt(kv[cc, 1], do2[...])
            for sl in lanes:
                p = sb[cc, :, sl] * stat[1, :, sl]
                pb[:, sl] = p.astype(BF16)
                db[:, sl] = (p * (dp[:, sl] - stat[2, :, sl])).astype(BF16)
            own[zz, 0, x] = SCALE * nn(db[...], q2[...])
            own[zz, 1, x] = nn(pb[...], do2[...])
            dqt[...] += tn(kv[cc, 0], db[...])
            return carry

        lax.fori_loop(0, 2, one, 0)

    first_hop = {(0, 1): up, (0, -1): dn, (1, 1): dn, (1, -1): up}
    slots = {1: rp, -1: rm}

    def pass_on(i, way, hop):
        zz = at_z(way * hop)
        total = own[zz, i]
        if hop < first_hop[i, way]:
            slot = slots[way].at[i, hop]
            arrive(("kvg", i, way, hop + 1), slot)
            total = total + slot[...].astype(F32)
        snd[zz, i] = total.astype(BF16)
        send(("kvg", i, way, hop), snd.at[zz, i], slots[way].at[i, hop - 1], zdev(way))

    half = ntp // 2
    per_piece = DC // CW

    def weight_part(part, base, out):
        piece = base * half + part
        for head in range(2):
            rows = slice(head * HD, (head + 1) * HD)
            res = nn(att[head], gb[piece])
            for j in range(per_piece):
                out[part * per_piece + j, rows] = res[:, j * CW:(j + 1) * CW].astype(out.dtype)

    def weight_other():
        arrive("att", att.at[o])

        def one(part, carry):
            weight_part(part, 1 - d, gws)
            return carry

        lax.fori_loop(0, half, one, 0)
        send("gw", gws, gwr, core)

    def weight_own():
        def one(part, carry):
            weight_part(part, d, gwo)
            return carry

        lax.fori_loop(0, half, one, 0)

    gslots = {1: gp, -1: gm}

    def weight_sum(zz, x):
        return gwo[2 * zz + x] + gwr[2 * zz + x].astype(F32)

    def weight_far():
        zz = at_z(up)
        for x, way in ((0, 1), (1, -1)):
            gsn[zz, x] = weight_sum(zz, x).astype(BF16)
            send(("gwz", way, up), gsn.at[zz, x], gslots[way].at[up - 1, x], zdev(way))

    def weight_arrive(way, hop):
        if hop == up:
            x = 0 if way == 1 else 1
            arrive(("gwz", way, hop), gslots[way].at[hop - 1, x])
            return [x]
        arrive(("gwz", way, hop), gslots[way].at[hop - 1])
        return [0, 1]

    def weight_pass(way, hop):
        zz = at_z(way * hop)
        halves = weight_arrive(way, hop + 1)
        for x in range(2):
            total = weight_sum(zz, x)
            if x in halves:
                total = total + gslots[way][hop, x].astype(F32)
            gsn[zz, x] = total.astype(BF16)
        send(("gwz", way, hop), gsn.at[zz], gslots[way].at[hop - 1], zdev(way))

    if nz > 1:
        gradients(at_z(up))
        pass_on(0, 1, up)
        pass_on(1, -1, up)
    if dn:
        gradients(at_z(dn))
        gradients(at_z(-dn))
    weight_other()
    late = []
    for hop in range(dn, 0, -1):
        if hop < dn:
            gradients(at_z(hop))
            gradients(at_z(-hop))
        for i in ((1, 0) if hop == dn else (0, 1)):
            pass_on(i, 1, hop)
            pass_on(1 - i, -1, hop)
        if hop == dn:
            weight_own()
        elif hop == dn - 1:
            arrive("gw", gwr)
            weight_far()
        else:
            weight_pass(1, hop + 2)
            weight_pass(-1, hop + 2)
    gradients(z)
    if dn == 0:
        weight_own()
    if dn < 2:
        arrive("gw", gwr)
        if nz > 1:
            weight_far()
        rest = range(dn, 0, -1)
    else:
        rest = range(2, 0, -1)

    dqb[...] = jnp.transpose(SCALE * dqt[...]).astype(BF16)
    send("dq", dqb.at[orows], dq_hbm.at[0, :, hcols], partner)
    out_q = local(2, dqb.at[hrows], dq_hbm.at[0, :, hcols])

    if len(rest) and dn:
        weight_pass(1, rest[0])
        weight_pass(-1, rest[0])

    outs = [out_q]
    for i, out in ((0, dk_hbm), (1, dv_hbm)):
        total = own[z, i]
        for way in (1, -1):
            if first_hop[i, way] > 0:
                arrive(("kvg", i, way, 1), slots[way].at[i, 0])
                total = total + slots[way][i, 0].astype(F32)
        fin[i] = total.astype(BF16)
        send(("fin", i), fin.at[i, o], out.at[0, :, hcols], partner)
        outs.append(local(i, fin.at[i, h], out.at[0, :, hcols]))

    for hop in rest[1:]:
        weight_pass(1, hop)
        weight_pass(-1, hop)
    tops = [weight_sum(z, 0), weight_sum(z, 1)]
    if nz > 1:
        for way in (1, -1):
            for x in weight_arrive(way, 1):
                tops[x] = tops[x] + gslots[way][0, x].astype(F32)
    gfin[0] = tops[0]
    gfin[1] = tops[1]
    gsn[z, 0] = gfin[o].astype(BF16)
    send("gwx", gsn.at[z, 0], gxr, partner)
    arrive("gwx", gxr)
    gout[...] = (gfin[h] + gxr[...].astype(F32)).astype(BF16)
    outs.append(local(3, gout, gw_hbm))

    arrive("dq", dq_hbm.at[0, :, ocols])
    arrive(("fin", 0), dk_hbm.at[0, :, ocols])
    arrive(("fin", 1), dv_hbm.at[0, :, ocols])
    for cp in outs:
        cp.wait()
    for cp in sent:
        cp.wait_send()
    assert len(sem.index) <= N_SEM


def per_device(nz, ny, q, k, v, g, w, pattern, offsets):
    T = q.shape[1]
    Q2 = 2 * T
    nctx, ntp = 2 * nz, 2 * ny
    DC, F = g.shape[2], w.shape[0]
    CW = w.shape[1] // (2 * nctx)
    deep = max(nz // 2, 1)
    V = pltpu.VMEM
    hbm = pl.BlockSpec(memory_space=pl.ANY)
    smem = pl.BlockSpec(memory_space=pltpu.SMEM)
    scratch = [
        V((nctx, 2, T, HD), BF16),
        V((Q2, HD), BF16),
        V((Q2, HD), BF16),
        V((ntp, T, DC), BF16),
        V(w.shape, BF16),
        V((T, F), F32),
        V((2, T, HD), BF16),
        V((nctx, T, 128), F32),
        V((nctx, 1, Q2), F32),
        V((nctx, T, Q2), F32),
        V((8, Q2), F32),
        V((8, Q2), F32),
        V((3, 1, Q2), F32),
        V((HD, Q2), F32),
        V((HD, Q2), BF16),
        V((2, HD, T), BF16),
        V((T, Q2), BF16),
        V((T, Q2), BF16),
        V((nz, 2, 2, T, HD), F32),
        V((nz, 2, 2, T, HD), BF16),
        V((2, deep, 2, T, HD), BF16),
        V((2, deep, 2, T, HD), BF16),
        V((HD, Q2), F32),
        V((Q2, HD), BF16),
        V((2, 2, T, HD), BF16),
        V((nctx, F, CW), BF16),
        V((nctx, F, CW), BF16),
        V((nctx, F, CW), F32),
        V((nz, 2, F, CW), BF16),
        V((deep, 2, F, CW), BF16),
        V((deep, 2, F, CW), BF16),
        V((2, F, CW), F32),
        V((F, CW), BF16),
        V((F, CW), BF16),
        pltpu.SemaphoreType.DMA((N_SEM,)),
        pltpu.SemaphoreType.DMA((N_SEM,)),
        pltpu.SemaphoreType.DMA((5,)),
    ]
    like = jax.ShapeDtypeStruct(q.shape, BF16)
    return pl.pallas_call(
        functools.partial(kernel, nz, ny),
        out_shape=(like, like, like, jax.ShapeDtypeStruct((F, CW), BF16)),
        in_specs=[smem, smem, hbm, hbm, hbm, hbm, hbm],
        out_specs=(hbm, hbm, hbm, hbm),
        scratch_shapes=scratch,
        compiler_params=pltpu.CompilerParams(
            collective_id=0, has_side_effects=True, vmem_limit_bytes=60 * 1024 * 1024
        ),
        name="attention_backward",
    )(pattern, offsets, q, k, v, g, w)


def solution(mesh):
    nz, ny = mesh.shape["ctx"] // 2, mesh.shape["tp"] // 2
    spec = P("dp", "ctx", "tp")
    return jax.shard_map(
        functools.partial(per_device, nz, ny),
        mesh=mesh,
        in_specs=(spec, spec, spec, spec, P("tp", None), P(), P()),
        out_specs=(spec, spec, spec, P("tp", ("dp", "ctx"))),
        check_vma=False,
    )
```

```python
import functools

import jax
import jax.numpy as jnp
from jax import lax
from jax.experimental import pallas as pl
from jax.experimental.pallas import tpu as pltpu
from jax.sharding import PartitionSpec as P

HD = 128
LOWEST = -1e30
SCALE = HD ** (-0.5)
LOG2E = 1.4426950408889634
MESH = pl.DeviceIdType.MESH
F32 = jnp.float32
BF16 = jnp.bfloat16


def nt(a, b):
    return lax.dot_general(a, b, (((1,), (1,)), ((), ())), preferred_element_type=F32)


def tn(a, b):
    return lax.dot_general(a, b, (((0,), (0,)), ((), ())), preferred_element_type=F32)


def nn(a, b):
    return jnp.dot(a, b, preferred_element_type=F32)


def any_of(flags):
    return functools.reduce(jnp.logical_or, flags)


class Sems:
    def __init__(self):
        self.index = {}

    def __getitem__(self, name):
        return self.index.setdefault(name, len(self.index))


N_SEM = 110


def arrival_times(flows):
    done, free = {}, {}
    left = dict(flows)
    while left:
        ready = []
        for name, (needs, delay, link, busy, wait) in left.items():
            if all(n in done for n in needs):
                start = max([done[n] for n in needs] + [0.0]) + delay
                ready.append((start, len(ready), name))
        start, _, name = min(ready)
        _, _, link, busy, wait = left.pop(name)
        begin = max(start, free.get(link, 0.0))
        free[link] = begin + busy
        done[name] = begin + busy + wait
    return done


def kernel(
    nz,
    ny,
    pat,
    offs,
    q_hbm,
    k_hbm,
    v_hbm,
    g_hbm,
    w_hbm,
    dq_hbm,
    dk_hbm,
    dv_hbm,
    gw_hbm,
    kv,
    q2,
    do2,
    gb,
    wv,
    gh,
    ghb,
    kb,
    qb,
    sb,
    mx,
    lr,
    stat,
    ot,
    ob,
    att,
    pb,
    db,
    own,
    snd,
    rp,
    rm,
    dqt,
    dqb,
    fin,
    gws,
    gwr,
    gwo,
    gxs,
    gxr,
    gsn,
    gp,
    gm,
    gout,
    ss,
    rs,
    ls,
):
    T = q_hbm.shape[1]
    Q2 = 2 * T
    nctx, ntp = 2 * nz, 2 * ny
    DC = g_hbm.shape[2]
    F = w_hbm.shape[0]
    CW = gw_hbm.shape[1]
    GB = offs.shape[0]
    up, dn = nz // 2, max(nz // 2 - 1, 0)
    yup, ydn = ny // 2, max(ny // 2 - 1, 0)
    lanes = [slice(i * 128, (i + 1) * 128) for i in range(Q2 // 128)]

    d = lax.axis_index("dp")
    c = lax.axis_index("ctx")
    t = lax.axis_index("tp")
    z, h = lax.div(c, 2), lax.rem(c, 2)
    y, xl = lax.div(t, 2), lax.rem(t, 2)
    o = 1 - h

    def at_z(step):
        return lax.rem(z + (step + nz), nz)

    def at_y(step):
        return lax.rem(y + (step + ny), ny)

    def zdev(step):
        return (d, at_z(step) * 2 + h, t)

    def ydev(step):
        return (d, c, at_y(step) * 2 + xl)

    partner = (d, 2 * z + o, t)
    xdev = (d, c, 2 * y + 1 - xl)
    core = (1 - d, c, t)
    hcols = pl.ds(pl.multiple_of(h * HD, HD), HD)
    ocols = pl.ds(pl.multiple_of(o * HD, HD), HD)
    hrows = pl.ds(pl.multiple_of(h * T, T), T)
    orows = pl.ds(pl.multiple_of(o * T, T), T)

    sem = Sems()
    sent = []

    def send(name, src, dst, dev):
        i = sem[name]
        cp = pltpu.make_async_remote_copy(
            src_ref=src, dst_ref=dst, send_sem=ss.at[i], recv_sem=rs.at[i],
            device_id=dev, device_id_type=MESH,
        )
        cp.start()
        sent.append(cp)

    def arrive(name, dst):
        i = sem[name]
        pltpu.make_async_remote_copy(
            src_ref=dst, dst_ref=dst, send_sem=ss.at[i], recv_sem=rs.at[i],
            device_id=partner, device_id_type=MESH,
        ).wait_recv()

    def local(i, src, dst):
        cp = pltpu.make_async_copy(src, dst, ls.at[i])
        cp.start()
        return cp

    load_k = local(0, k_hbm.at[0, :, hcols], kv.at[c, 0])
    load_v = local(1, v_hbm.at[0, :, hcols], kv.at[c, 1])
    load_q = local(2, q_hbm.at[0, :, hcols], q2.at[hrows])
    load_g = local(3, g_hbm.at[0], gb.at[t])
    load_w = local(4, w_hbm, wv)

    near = [partner, xdev, core]
    if nz > 1:
        near += [zdev(1), zdev(-1)]
    if ny > 1:
        near += [ydev(1), ydev(-1)]
    barrier = pltpu.get_barrier_semaphore()
    for dev in near:
        pl.semaphore_signal(barrier, inc=1, device_id=dev, device_id_type=MESH)
    pl.semaphore_wait(barrier, len(near))

    hops = {("a", 1): up, ("a", -1): dn, ("b", 1): dn, ("b", -1): up}

    def z_block(chain, step):
        return 2 * at_z(step) + (h if chain == "a" else o)

    def z_send(chain, way, hop, i):
        if hop < hops[chain, way]:
            block = kv.at[z_block(chain, -way * hop), i]
            send(("kv", chain, way, hop + 1, i), block, block, zdev(way))

    ghops = {("a", 1): yup, ("a", -1): ydn, ("b", 1): ydn, ("b", -1): yup}
    halves = [pl.ds(i * (T // 2), T // 2) for i in range(2)]

    def y_piece(chain, step):
        return 2 * at_y(step) + (xl if chain == "a" else 1 - xl)

    def y_send(chain, way, hop, i):
        if hop < ghops[chain, way]:
            piece = gb.at[y_piece(chain, -way * hop), halves[i]]
            src = g_hbm.at[0, halves[i]] if chain == "a" and hop == 0 else piece
            send(("g", chain, way, hop + 1, i), src, piece, ydev(way))

    def x_send(i):
        send(("gx", i), g_hbm.at[0, halves[i]], gb.at[t, halves[i]], xdev)

    x_send(0)
    for i in range(2):
        y_send("a", 1, 0, i)
        y_send("a", -1, 0, i)
    send("k", k_hbm.at[0, :, ocols], kv.at[c, 0], partner)
    send("v", v_hbm.at[0, :, ocols], kv.at[c, 1], partner)
    x_send(1)
    send("q", q_hbm.at[0, :, ocols], q2.at[hrows], partner)
    for i, load in ((0, load_k), (1, load_v)):
        load.wait()
        z_send("a", 1, 0, i)
        z_send("a", -1, 0, i)

    lane = lax.broadcasted_iota(jnp.int32, (1, Q2), 1)
    is_first = lane < T
    pos = jnp.where(is_first, lane, lane - T)
    b0 = 2 * z
    bvec = jnp.where(is_first, b0, b0 + 1)

    def both(ref, k):
        return jnp.where(is_first, ref[k, b0], ref[k, b0 + 1])

    row_global = any_of([pos == both(offs, g) for g in range(GB)])
    picks = [both(pat, r) for r in range(pat.shape[0])]
    for cc in range(nctx):
        seen = any_of([row_global, jnp.abs(bvec - cc) <= 1] + [pick == cc for pick in picks])
        qb[cc] = jnp.where(seen, 0.0, LOWEST)

    def key_bias(cc, carry):
        row = lax.broadcasted_iota(jnp.int32, (T, 128), 0)
        kb[cc] = jnp.where(any_of([row == offs[g, cc] for g in range(GB)]), 0.0, LOWEST)
        return carry

    lax.fori_loop(0, nctx, key_bias, 0)
    mx[...] = jnp.full_like(mx, LOWEST)
    gh[...] = jnp.zeros_like(gh)
    lr[...] = jnp.zeros_like(lr)
    ot[...] = jnp.zeros_like(ot)

    def score(cc):
        s = nt(kv[cc, 0], q2[...])
        bias = kb[cc]
        row_bias = qb[cc]
        for sl in lanes:
            part = s[:, sl] + jnp.maximum(bias, row_bias[:, sl])
            sb[cc, :, sl] = part
            mx[:, sl] = jnp.maximum(mx[:, sl], jnp.max(part.reshape(T // 8, 8, 128), axis=0))

    def project(tt):
        cols = pl.ds(pl.multiple_of(tt * DC, DC), DC)
        gh[...] += nt(gb[tt], wv[:, cols])

    group_of = {step: max(abs(step) - 1, 0) for step in range(-dn, up + 1)}
    n_group = max(group_of.values()) + 1
    TOTAL, DOT, FACTOR = n_group, n_group + 1, n_group + 2

    def weigh(j):
        stat[j] = jnp.max(mx[...], axis=0, keepdims=True)
        if j:
            scale = jnp.exp2((stat[j - 1] - stat[j]) * (SCALE * LOG2E))
            ot[...] = ot[...] * scale
            lr[...] = lr[...] * scale

        def one(cc):
            for sl in lanes:
                e = jnp.exp2((sb[cc, :, sl] - stat[j, :, sl]) * (SCALE * LOG2E))
                sb[cc, :, sl] = e
                lr[:, sl] += jnp.sum(e.reshape(T // 8, 8, 128), axis=0)
                pb[:, sl] = e.astype(BF16)
            ot[...] += tn(kv[cc, 1], pb[...])

        for step in [step for step, group in group_of.items() if group == j]:

            def pair(x, carry, step=step):
                one(2 * at_z(step) + x)
                return carry

            lax.fori_loop(0, 2, pair, 0)

    ready = {"q": False, "blocks": []}
    missing = {j: sum(4 for group in group_of.values() if group == j) for j in range(n_group)}

    def landed(step, count=1):
        missing[group_of[step]] -= count
        while missing and ready["q"] and missing[min(missing)] == 0:
            j = min(missing)
            del missing[j]
            weigh(j)

    def scores_of(cc):
        if ready["q"]:
            score(cc)
        else:
            ready["blocks"].append(cc)

    def on_own():
        load_g.wait()
        load_w.wait()
        project(t)
        scores_of(z_block("a", 0))
        landed(0, 2)

    def on_q():
        load_q.wait()
        arrive("q", q2.at[orows])
        ready["q"] = True
        for cc in ready["blocks"]:
            score(cc)
        landed(0, 0)

    def on_pair(i):
        pair = z_block("b", 0)
        arrive("kv"[i], kv.at[pair, i])
        z_send("b", 1, 0, i)
        z_send("b", -1, 0, i)
        if i == 0:
            scores_of(pair)
        landed(0)

    def on_gx(i):
        piece = y_piece("b", 0)
        arrive(("gx", i), gb.at[piece, halves[i]])
        y_send("b", 1, 0, i)
        y_send("b", -1, 0, i)
        if i:
            project(piece)

    def on_kv(chain, way, hop, i):
        step = -way * hop
        if step == -up:
            step = up
        block = z_block(chain, step)
        arrive(("kv", chain, way, hop, i), kv.at[block, i])
        z_send(chain, way, hop, i)
        if i == 0:
            scores_of(block)
        landed(step)

    def on_g(chain, way, hop, i):
        piece = y_piece(chain, -way * hop)
        arrive(("g", chain, way, hop, i), gb.at[piece, halves[i]])
        y_send(chain, way, hop, i)
        if i:
            project(piece)

    us = 2.0 / 88e3
    kv_us, g_us = T * HD * 2 * us, T * DC * us
    flows = {("gx", 0): ((), 0, "x", g_us, 1.8)}
    events = {("gx", 0): functools.partial(on_gx, 0)}
    for i in range(2):
        flows["kv"[i]] = ((), 0, "x", kv_us, 2.6)
        events["kv"[i]] = functools.partial(on_pair, i)
    flows["gx", 1] = ((), 0, "x", g_us, 1.8)
    events["gx", 1] = functools.partial(on_gx, 1)
    flows["q"] = ((), 0, "x", kv_us, 2.6)
    events["q"] = on_q
    for i in range(2):
        for (chain, way), count in hops.items():
            for hop in range(1, count + 1):
                name = ("kv", chain, way, hop, i)
                first = () if chain == "a" else ("kv"[i],)
                needs = (("kv", chain, way, hop - 1, i),) if hop > 1 else first
                flows[name] = (needs, 0.1, ("z", way), kv_us, 1.9)
                events[name] = functools.partial(on_kv, chain, way, hop, i)
        for (chain, way), count in ghops.items():
            for hop in range(1, count + 1):
                name = ("g", chain, way, hop, i)
                first = () if chain == "a" else (("gx", i),)
                needs = (("g", chain, way, hop - 1, i),) if hop > 1 else first
                flows[name] = (needs, 0.1, ("y", way), g_us, 1.8)
                events[name] = functools.partial(on_g, chain, way, hop, i)
    times = arrival_times(flows)

    def gather(names):
        for name in sorted(names, key=times.get):
            events[name]()

    last_g = max([times[name] for name in events if name[0] in ("g", "gx")])
    on_own()
    gather([name for name in events if times[name] <= last_g])
    ghb[0] = gh[:, :HD].astype(BF16)
    ghb[1] = gh[:, HD:].astype(BF16)
    send("do", ghb.at[o], do2.at[hrows], partner)
    do2[hrows, :] = ghb[h]
    gather([name for name in events if times[name] > last_g])

    inverse = 1.0 / jnp.sum(lr[...], axis=0, keepdims=True)
    low = (ot[...] * inverse).astype(BF16)
    ob[...] = low
    send("att", ob.at[:, orows], att.at[h], partner)
    att[h] = ob[:, hrows]
    for j in range(n_group):
        back = jnp.exp2((stat[j] - stat[n_group - 1]) * (SCALE * LOG2E))
        stat[FACTOR + j] = inverse * back
    arrive("do", do2.at[orows])
    do_t = jnp.transpose(do2[...].astype(F32))
    stat[DOT] = jnp.sum(do_t * low.astype(F32), axis=0, keepdims=True)
    dqt[...] = jnp.zeros_like(dqt)

    def gradients(step):
        zz = at_z(step)
        factor = stat.at[FACTOR + group_of[step]]

        def one(x, carry):
            cc = 2 * zz + x
            dp = nt(kv[cc, 1], do2[...])
            for sl in lanes:
                p = sb[cc, :, sl] * factor[:, sl]
                pb[:, sl] = p.astype(BF16)
                db[:, sl] = (p * (dp[:, sl] - stat[DOT, :, sl])).astype(BF16)
            own[zz, 0, x] = SCALE * nn(db[...], q2[...])
            own[zz, 1, x] = nn(pb[...], do2[...])
            dqt[...] += tn(kv[cc, 0], db[...])
            return carry

        lax.fori_loop(0, 2, one, 0)

    first_hop = {(0, 1): up, (0, -1): dn, (1, 1): dn, (1, -1): up}
    slots = {1: rp, -1: rm}

    def pass_on(i, way, hop):
        zz = at_z(way * hop)
        total = own[zz, i]
        if hop < first_hop[i, way]:
            slot = slots[way].at[i, hop]
            arrive(("kvg", i, way, hop + 1), slot)
            total = total + slot[...].astype(F32)
        snd[zz, i] = total.astype(BF16)
        send(("kvg", i, way, hop), snd.at[zz, i], slots[way].at[i, hop - 1], zdev(way))

    half = ntp // 2
    per_piece = DC // CW

    def weight_part(part, base, out):
        piece = base * half + part
        for head in range(2):
            rows = slice(head * HD, (head + 1) * HD)
            res = nn(att[head], gb[piece])
            for j in range(per_piece):
                out[part * per_piece + j, rows] = res[:, j * CW:(j + 1) * CW].astype(out.dtype)

    def weight_other():
        arrive("att", att.at[o])
        for part in range(half):
            weight_part(part, 1 - d, gws)
            block = pl.ds(part * per_piece, per_piece)
            send(("gw", part), gws.at[block], gwr.at[block], core)

    def weight_own():
        def one(part, carry):
            weight_part(part, d, gwo)
            return carry

        lax.fori_loop(0, half, one, 0)

    def weight_cross():
        for part in range(half):
            arrive(("gw", part), gwr.at[pl.ds(part * per_piece, per_piece)])
        for step in order:
            zz = at_z(step)
            gxs[zz] = (gwo[2 * zz + o] + gwr[2 * zz + o].astype(F32)).astype(BF16)
            send(("gwx", step), gxs.at[zz], gxr.at[zz], partner)

    order = [up] if nz > 1 else []
    for hop in range(dn, 0, -1):
        order += [hop, -hop]
    order += [0]
    gslots = {1: gp, -1: gm}
    tops = {1: pl.ds(0, F // 2), -1: pl.ds(F // 2, F // 2)}

    def weight_total(step):
        zz = at_z(step)
        arrive(("gwx", step), gxr.at[zz])
        gwo[2 * zz + h] = gwo[2 * zz + h] + gwr[2 * zz + h].astype(F32) + gxr[zz].astype(F32)

    def weight_add(zz, way, hop):
        rows = tops[way] if hop == up else pl.ds(0, F)
        slot = gslots[way].at[hop - 1, rows]
        arrive(("gwz", way, hop), slot)
        gwo[2 * zz + h, rows] = gwo[2 * zz + h, rows] + slot[...].astype(F32)

    def weight_far():
        weight_total(up)
        zz = at_z(up)
        gsn[zz] = gwo[2 * zz + h].astype(BF16)
        for way in (1, -1):
            send(("gwz", way, up), gsn.at[zz, tops[way]], gslots[way].at[up - 1, tops[way]], zdev(way))

    def weight_pass(way, hop):
        weight_total(way * hop)
        zz = at_z(way * hop)
        weight_add(zz, way, hop + 1)
        gsn[zz] = gwo[2 * zz + h].astype(BF16)
        send(("gwz", way, hop), gsn.at[zz], gslots[way].at[hop - 1], zdev(way))

    def gradient_pair(hop):
        gradients(hop)
        gradients(-hop)

    def finish(i):
        out = (dk_hbm, dv_hbm)[i]
        total = own[z, i]
        for way in (1, -1):
            if first_hop[i, way] > 0:
                arrive(("kvg", i, way, 1), slots[way].at[i, 0])
                total = total + slots[way][i, 0].astype(F32)
        fin[i] = total.astype(BF16)
        send(("fin", i), fin.at[i, o], out.at[0, :, hcols], partner)
        outs.append(local(i, fin.at[i, h], out.at[0, :, hcols]))

    outs = []

    def finish_q():
        dqb[...] = jnp.transpose(SCALE * dqt[...]).astype(BF16)
        send("dq", dqb.at[orows], dq_hbm.at[0, :, hcols], partner)
        outs.append(local(2, dqb.at[hrows], dq_hbm.at[0, :, hcols]))

    def finish_weight():
        weight_total(0)
        if nz > 1:
            weight_add(z, 1, 1)
            weight_add(z, -1, 1)
        gout[...] = gwo[2 * z + h].astype(BF16)
        outs.append(local(3, gout, gw_hbm))

    part = functools.partial
    if nz > 1:
        gradients(up)
        pass_on(0, 1, up)
        pass_on(1, -1, up)
    if dn:
        gradient_pair(dn)
        pass_on(1, 1, dn)
        pass_on(0, -1, dn)
    work = [part(gradient_pair, hop) for hop in range(dn - 1, 0, -1)]
    work += [part(gradients, 0), finish_q]
    if work:
        work.pop(0)()
    weight_other()
    weight_own()
    if dn:
        pass_on(0, 1, dn)
        pass_on(1, -1, dn)
    while work:
        work.pop(0)()
    weight_cross()
    tasks = []
    for hop in range(dn - 1, 0, -1):
        tasks += [part(pass_on, 1, 1, hop), part(pass_on, 0, -1, hop)]
        tasks += [part(pass_on, 0, 1, hop), part(pass_on, 1, -1, hop)]
    tasks += [part(finish, 1), part(finish, 0)] if dn else [part(finish, 0), part(finish, 1)]
    more = [weight_far] if nz > 1 else []
    for hop in range(dn, 0, -1):
        more += [part(weight_pass, 1, hop), part(weight_pass, -1, hop)]
    for i, task in enumerate(tasks):
        task()
        if i >= 3 and more and i % 2 == 1:
            for task in more[:1 if more[0] is weight_far else 2]:
                task()
                more.pop(0)
    for task in more:
        task()
    finish_weight()

    arrive("dq", dq_hbm.at[0, :, ocols])
    arrive(("fin", 0), dk_hbm.at[0, :, ocols])
    arrive(("fin", 1), dv_hbm.at[0, :, ocols])
    for cp in outs:
        cp.wait()
    for cp in sent:
        cp.wait_send()
    assert len(sem.index) <= N_SEM


def hand_on(*refs):
    n = (len(refs) - 1) // 3
    ins, outs, bufs, sems = refs[:n], refs[n:2 * n], refs[2 * n:3 * n], refs[3 * n]
    reads = [pltpu.make_async_copy(a, b, sems.at[i]) for i, (a, b) in enumerate(zip(ins, bufs))]
    writes = [pltpu.make_async_copy(a, b, sems.at[n + i]) for i, (a, b) in enumerate(zip(bufs, outs))]
    for cp in reads:
        cp.start()
    for read, write in zip(reads, writes):
        read.wait()
        write.start()
    for cp in writes:
        cp.wait()


def per_device(nz, ny, q, k, v, g, w, pattern, offsets):
    T = q.shape[1]
    Q2 = 2 * T
    nctx, ntp = 2 * nz, 2 * ny
    DC, F = g.shape[2], w.shape[0]
    CW = w.shape[1] // (2 * nctx)
    deep = max(nz // 2, 1)
    V = pltpu.VMEM
    hbm = pl.BlockSpec(memory_space=pl.ANY)
    smem = pl.BlockSpec(memory_space=pltpu.SMEM)
    scratch = [
        V((nctx, 2, T, HD), BF16),
        V((Q2, HD), BF16),
        V((Q2, HD), BF16),
        V((ntp, T, DC), BF16),
        V(w.shape, BF16),
        V((T, F), F32),
        V((2, T, HD), BF16),
        V((nctx, T, 128), F32),
        V((nctx, 1, Q2), F32),
        V((nctx, T, Q2), F32),
        V((8, Q2), F32),
        V((8, Q2), F32),
        V((2 * deep + 4, 1, Q2), F32),
        V((HD, Q2), F32),
        V((HD, Q2), BF16),
        V((2, HD, T), BF16),
        V((T, Q2), BF16),
        V((T, Q2), BF16),
        V((nz, 2, 2, T, HD), F32),
        V((nz, 2, 2, T, HD), BF16),
        V((2, deep, 2, T, HD), BF16),
        V((2, deep, 2, T, HD), BF16),
        V((HD, Q2), F32),
        V((Q2, HD), BF16),
        V((2, 2, T, HD), BF16),
        V((nctx, F, CW), BF16),
        V((nctx, F, CW), BF16),
        V((nctx, F, CW), F32),
        V((nz, F, CW), BF16),
        V((nz, F, CW), BF16),
        V((nz, F, CW), BF16),
        V((deep, F, CW), BF16),
        V((deep, F, CW), BF16),
        V((F, CW), BF16),
        pltpu.SemaphoreType.DMA((N_SEM,)),
        pltpu.SemaphoreType.DMA((N_SEM,)),
        pltpu.SemaphoreType.DMA((5,)),
    ]
    like = jax.ShapeDtypeStruct(q.shape, BF16)
    shapes = (like, like, like, jax.ShapeDtypeStruct((F, CW), BF16))
    results = pl.pallas_call(
        functools.partial(kernel, nz, ny),
        out_shape=shapes,
        in_specs=[smem, smem, hbm, hbm, hbm, hbm, hbm],
        out_specs=(hbm, hbm, hbm, hbm),
        scratch_shapes=scratch,
        compiler_params=pltpu.CompilerParams(
            collective_id=0, has_side_effects=True, vmem_limit_bytes=60 * 1024 * 1024
        ),
        name="attention_backward",
    )(pattern.T, offsets.T, q, k, v, g, w)
    return tuple(
        pl.pallas_call(
            hand_on,
            out_shape=shapes,
            in_specs=[hbm] * 4,
            out_specs=(hbm,) * 4,
            scratch_shapes=[V(s.shape, BF16) for s in shapes] + [pltpu.SemaphoreType.DMA((8,))],
            name="hand_on",
        )(*results)
    )


def solution(mesh):
    nz, ny = mesh.shape["ctx"] // 2, mesh.shape["tp"] // 2
    spec = P("dp", "ctx", "tp")
    return jax.shard_map(
        functools.partial(per_device, nz, ny),
        mesh=mesh,
        in_specs=(spec, spec, spec, spec, P("tp", None), P(), P()),
        out_specs=(spec, spec, spec, P("tp", ("dp", "ctx"))),
        check_vma=False,
    )
```

```python
import functools

import jax
import jax.numpy as jnp
from jax import lax
from jax.experimental import pallas as pl
from jax.experimental.pallas import tpu as pltpu
from jax.sharding import PartitionSpec as P

HD = 128
LOWEST = -1e30
SCALE = HD ** (-0.5)
LOG2E = 1.4426950408889634
MESH = pl.DeviceIdType.MESH
F32 = jnp.float32
BF16 = jnp.bfloat16


def nt(a, b):
    return lax.dot_general(a, b, (((1,), (1,)), ((), ())), preferred_element_type=F32)


def tn(a, b):
    return lax.dot_general(a, b, (((0,), (0,)), ((), ())), preferred_element_type=F32)


def nn(a, b):
    return jnp.dot(a, b, preferred_element_type=F32)


def any_of(flags):
    return functools.reduce(jnp.logical_or, flags)


class Sems:
    def __init__(self):
        self.index = {}

    def __getitem__(self, name):
        return self.index.setdefault(name, len(self.index))


N_SEM = 140


def arrival_times(flows):
    done, free = {}, {}
    left = dict(flows)
    while left:
        ready = []
        for name, (needs, delay, link, busy, wait) in left.items():
            if all(n in done for n in needs):
                start = max([done[n] for n in needs] + [0.0]) + delay
                ready.append((start, len(ready), name))
        start, _, name = min(ready)
        _, _, link, busy, wait = left.pop(name)
        begin = max(start, free.get(link, 0.0))
        free[link] = begin + busy
        done[name] = begin + busy + wait
    return done


def kernel(
    nz,
    ny,
    pat,
    offs,
    q_hbm,
    k_hbm,
    v_hbm,
    g_hbm,
    w_hbm,
    dq_hbm,
    dk_hbm,
    dv_hbm,
    gw_hbm,
    kv,
    q2,
    do2,
    gb,
    wv,
    gh,
    ghb,
    kb,
    qb,
    sb,
    mx,
    lr,
    stat,
    ot,
    ob,
    att,
    pb,
    db,
    own,
    snd,
    rp,
    rm,
    dqt,
    dqb,
    fin,
    gws,
    gwr,
    gwo,
    gxs,
    gxr,
    gsn,
    gp,
    gm,
    gout,
    ss,
    rs,
    ls,
):
    T = q_hbm.shape[1]
    Q2 = 2 * T
    nctx, ntp = 2 * nz, 2 * ny
    DC = g_hbm.shape[2]
    F = w_hbm.shape[0]
    CW = gw_hbm.shape[1]
    GB = offs.shape[0]
    up, dn = nz // 2, max(nz // 2 - 1, 0)
    yup, ydn = ny // 2, max(ny // 2 - 1, 0)
    lanes = [slice(i * 128, (i + 1) * 128) for i in range(Q2 // 128)]

    d = lax.axis_index("dp")
    c = lax.axis_index("ctx")
    t = lax.axis_index("tp")
    z, h = lax.div(c, 2), lax.rem(c, 2)
    y, xl = lax.div(t, 2), lax.rem(t, 2)
    o = 1 - h

    def at_z(step):
        return lax.rem(z + (step + nz), nz)

    def at_y(step):
        return lax.rem(y + (step + ny), ny)

    def zdev(step, column=None):
        return (d, at_z(step) * 2 + (h if column is None else column), t)

    def ydev(step):
        return (d, c, at_y(step) * 2 + xl)

    partner = (d, 2 * z + o, t)
    xdev = (d, c, 2 * y + 1 - xl)
    core = (1 - d, c, t)
    hcols = pl.ds(pl.multiple_of(h * HD, HD), HD)
    ocols = pl.ds(pl.multiple_of(o * HD, HD), HD)
    hrows = pl.ds(pl.multiple_of(h * T, T), T)
    orows = pl.ds(pl.multiple_of(o * T, T), T)

    sem = Sems()
    sent = []

    def send(name, src, dst, dev):
        i = sem[name]
        cp = pltpu.make_async_remote_copy(
            src_ref=src, dst_ref=dst, send_sem=ss.at[i], recv_sem=rs.at[i],
            device_id=dev, device_id_type=MESH,
        )
        cp.start()
        sent.append(cp)

    def arrive(name, dst):
        i = sem[name]
        pltpu.make_async_remote_copy(
            src_ref=dst, dst_ref=dst, send_sem=ss.at[i], recv_sem=rs.at[i],
            device_id=partner, device_id_type=MESH,
        ).wait_recv()

    def local(i, src, dst):
        cp = pltpu.make_async_copy(src, dst, ls.at[i])
        cp.start()
        return cp

    load_k = local(0, k_hbm.at[0, :, hcols], kv.at[c, 0])
    load_v = local(1, v_hbm.at[0, :, hcols], kv.at[c, 1])
    load_q = local(2, q_hbm.at[0, :, hcols], q2.at[hrows])
    load_g = local(3, g_hbm.at[0], gb.at[t])
    load_w = local(4, w_hbm, wv)

    near = [partner, xdev, core]
    if nz > 1:
        near += [zdev(1), zdev(-1)]
    if ny > 1:
        near += [ydev(1), ydev(-1)]
    barrier = pltpu.get_barrier_semaphore()
    for dev in near:
        pl.semaphore_signal(barrier, inc=1, device_id=dev, device_id_type=MESH)
    pl.semaphore_wait(barrier, len(near))

    halves = [pl.ds(i * (T // 2), T // 2) for i in range(2)]

    hops = {("a", 1): up, ("a", -1): dn, ("b", 1): dn, ("b", -1): up}

    def z_block(chain, step):
        return 2 * at_z(step) + (h if chain == "a" else o)

    def z_send(chain, way, hop, i, j):
        if hop < hops[chain, way]:
            block = kv.at[z_block(chain, -way * hop), i, halves[j]]
            send(("kv", chain, way, hop + 1, i, j), block, block, zdev(way))

    def y_piece(chain, step):
        return 2 * at_y(step) + (xl if chain == "a" else 1 - xl)

    def y_goes(chain, way, hop, i):
        if hop < yup:
            return True
        return hop == yup and chain == "a" and i == (0 if way == 1 else 1)

    def y_send(chain, way, hop, i):
        if y_goes(chain, way, hop + 1, i):
            piece = gb.at[y_piece(chain, -way * hop), halves[i]]
            src = g_hbm.at[0, halves[i]] if chain == "a" and hop == 0 else piece
            send(("g", chain, way, hop + 1, i), src, piece, ydev(way))

    def x_send(i):
        send(("gx", i), g_hbm.at[0, halves[i]], gb.at[t, halves[i]], xdev)

    for i, src in ((0, k_hbm), (1, v_hbm)):
        for j in range(2):
            send(("kv"[i], j), src.at[0, halves[j], ocols], kv.at[c, i, halves[j]], partner)
    for i in range(2):
        y_send("a", 1, 0, i)
        y_send("a", -1, 0, 1 - i)
    x_send(0)
    x_send(1)
    send("q", q_hbm.at[0, :, ocols], q2.at[hrows], partner)
    for i, load in ((0, load_k), (1, load_v)):
        load.wait()
        for j in range(2):
            z_send("a", 1, 0, i, j)
            z_send("a", -1, 0, i, j)

    lane = lax.broadcasted_iota(jnp.int32, (1, Q2), 1)
    is_first = lane < T
    pos = jnp.where(is_first, lane, lane - T)
    b0 = 2 * z
    bvec = jnp.where(is_first, b0, b0 + 1)

    def both(ref, k):
        return jnp.where(is_first, ref[k, b0], ref[k, b0 + 1])

    row_global = any_of([pos == both(offs, g) for g in range(GB)])
    picks = [both(pat, r) for r in range(pat.shape[0])]
    for cc in range(nctx):
        seen = any_of([row_global, jnp.abs(bvec - cc) <= 1] + [pick == cc for pick in picks])
        qb[cc] = jnp.where(seen, 0.0, LOWEST)

    def key_bias(cc, carry):
        row = lax.broadcasted_iota(jnp.int32, (T, 128), 0)
        kb[cc] = jnp.where(any_of([row == offs[g, cc] for g in range(GB)]), 0.0, LOWEST)
        return carry

    lax.fori_loop(0, nctx, key_bias, 0)
    mx[...] = jnp.full_like(mx, LOWEST)
    gh[...] = jnp.zeros_like(gh)
    lr[...] = jnp.zeros_like(lr)
    ot[...] = jnp.zeros_like(ot)

    def score(cc):
        s = nt(kv[cc, 0], q2[...])
        bias = kb[cc]
        row_bias = qb[cc]
        for sl in lanes:
            part = s[:, sl] + jnp.maximum(bias, row_bias[:, sl])
            sb[cc, :, sl] = part
            mx[:, sl] = jnp.maximum(mx[:, sl], jnp.max(part.reshape(T // 8, 8, 128), axis=0))

    def project(tt):
        cols = pl.ds(pl.multiple_of(tt * DC, DC), DC)
        gh[...] += nt(gb[tt], wv[:, cols])

    group_of = {step: max(abs(step) - 1, 0) for step in range(-dn, up + 1)}
    n_group = max(group_of.values()) + 1
    TOTAL, DOT, FACTOR = n_group, n_group + 1, n_group + 2

    def weigh(j):
        stat[j] = jnp.max(mx[...], axis=0, keepdims=True)
        if j:
            scale = jnp.exp2((stat[j - 1] - stat[j]) * (SCALE * LOG2E))
            ot[...] = ot[...] * scale
            lr[...] = lr[...] * scale

        def one(cc):
            for sl in lanes:
                e = jnp.exp2((sb[cc, :, sl] - stat[j, :, sl]) * (SCALE * LOG2E))
                sb[cc, :, sl] = e
                lr[:, sl] += jnp.sum(e.reshape(T // 8, 8, 128), axis=0)
                pb[:, sl] = e.astype(BF16)
            ot[...] += tn(kv[cc, 1], pb[...])

        for step in [step for step, group in group_of.items() if group == j]:

            def pair(x, carry, step=step):
                one(2 * at_z(step) + x)
                return carry

            lax.fori_loop(0, 2, pair, 0)

    ready = {"q": False, "blocks": []}
    missing = {j: sum(8 for group in group_of.values() if group == j) for j in range(n_group)}

    def landed(step, count=1):
        missing[group_of[step]] -= count
        while missing and ready["q"] and missing[min(missing)] == 0:
            j = min(missing)
            del missing[j]
            weigh(j)

    def scores_of(cc):
        if ready["q"]:
            score(cc)
        else:
            ready["blocks"].append(cc)

    def on_own():
        load_g.wait()
        load_w.wait()
        project(t)
        scores_of(z_block("a", 0))
        landed(0, 4)

    def on_q():
        load_q.wait()
        arrive("q", q2.at[orows])
        ready["q"] = True
        for cc in ready["blocks"]:
            score(cc)
        landed(0, 0)

    def on_pair(i, j):
        pair = z_block("b", 0)
        arrive(("kv"[i], j), kv.at[pair, i, halves[j]])
        z_send("b", 1, 0, i, j)
        z_send("b", -1, 0, i, j)
        if i == 0 and j == 1:
            scores_of(pair)
        landed(0)

    def on_gx(i):
        piece = y_piece("b", 0)
        arrive(("gx", i), gb.at[piece, halves[i]])
        y_send("b", 1, 0, i)
        y_send("b", -1, 0, i)
        if i:
            project(piece)

    def on_kv(chain, way, hop, i, j):
        step = -way * hop
        if step == -up:
            step = up
        block = z_block(chain, step)
        arrive(("kv", chain, way, hop, i, j), kv.at[block, i, halves[j]])
        z_send(chain, way, hop, i, j)
        if i == 0 and j == 1:
            scores_of(block)
        landed(step)

    pieces = {}

    def piece_half(chain, step):
        step = yup if step == -yup else step
        pieces[chain, step] = pieces.get((chain, step), 0) + 1
        if pieces[chain, step] == 2:
            project(y_piece(chain, step))

    def on_g(chain, way, hop, i):
        step = yup if hop == yup else -way * hop
        here = gb.at[y_piece(chain, step), halves[i]]
        arrive(("g", chain, way, hop, i), here)
        y_send(chain, way, hop, i)
        if hop == yup:
            send(("gc", i), here, here, xdev)
        piece_half(chain, step)

    def on_gc(i):
        arrive(("gc", i), gb.at[y_piece("b", yup), halves[i]])
        piece_half("b", yup)

    us = 2.0 / 88e3
    kv_us, g_us = T * HD * 2 * us, T * DC * us
    part = functools.partial
    flows, events = {}, {}

    def flow(name, needs, delay, link, busy, wait, event):
        flows[name] = (needs, delay, link, busy, wait)
        events[name] = event

    for i in range(2):
        for j in range(2):
            flow(("kv"[i], j), (), 0, "x", kv_us / 2, 2.6, part(on_pair, i, j))
    for i in range(2):
        flow(("gx", i), (), 0, "x", g_us, 1.8, part(on_gx, i))
    flow("q", (), 0, "x", kv_us, 2.6, on_q)
    for i in range(2):
        for (chain, way), count in hops.items():
            for hop, j in [(hop, j) for hop in range(1, count + 1) for j in range(2)]:
                first = () if chain == "a" else (("kv"[i], j),)
                needs = (("kv", chain, way, hop - 1, i, j),) if hop > 1 else first
                name = ("kv", chain, way, hop, i, j)
                flow(name, needs, 0.1, ("z", way), kv_us / 2, 2.2, part(on_kv, chain, way, hop, i, j))
        for chain in "ab":
            for way in (1, -1):
                for hop in range(1, yup + 1):
                    if y_goes(chain, way, hop, i):
                        first = () if chain == "a" else (("gx", i),)
                        needs = (("g", chain, way, hop - 1, i),) if hop > 1 else first
                        late = 0.2 if i == (0 if way == -1 else 1) else 0.1
                        name = ("g", chain, way, hop, i)
                        flow(name, needs, late, ("y", way), g_us, 1.8, part(on_g, chain, way, hop, i))
                        if hop == yup:
                            flow(("gc", i), (name,), 0.1, "x", g_us, 1.8, part(on_gc, i))
    times = arrival_times(flows)

    def gather(names):
        for name in sorted(names, key=times.get):
            events[name]()

    last_g = max([times[name] for name in events if name[0] in ("g", "gx", "gc")])
    on_own()
    gather([name for name in events if times[name] <= last_g])
    ghb[0] = gh[:, :HD].astype(BF16)
    ghb[1] = gh[:, HD:].astype(BF16)
    send("do", ghb.at[o], do2.at[hrows], partner)
    do2[hrows, :] = ghb[h]
    gather([name for name in events if times[name] > last_g])

    inverse = 1.0 / jnp.sum(lr[...], axis=0, keepdims=True)
    low = (ot[...] * inverse).astype(BF16)
    ob[...] = low
    send("att", ob.at[:, orows], att.at[h], partner)
    att[h] = ob[:, hrows]
    for j in range(n_group):
        back = jnp.exp2((stat[j] - stat[n_group - 1]) * (SCALE * LOG2E))
        stat[FACTOR + j] = inverse * back
    arrive("do", do2.at[orows])
    do_t = jnp.transpose(do2[...].astype(F32))
    stat[DOT] = jnp.sum(do_t * low.astype(F32), axis=0, keepdims=True)
    dqt[...] = jnp.zeros_like(dqt)

    def gradients(step):
        zz = at_z(step)
        factor = stat.at[FACTOR + group_of[step]]

        def one(x, carry):
            cc = 2 * zz + x
            dp = nt(kv[cc, 1], do2[...])
            for sl in lanes:
                p = sb[cc, :, sl] * factor[:, sl]
                pb[:, sl] = p.astype(BF16)
                db[:, sl] = (p * (dp[:, sl] - stat[DOT, :, sl])).astype(BF16)
            own[zz, 0, x] = SCALE * nn(db[...], q2[...])
            own[zz, 1, x] = nn(pb[...], do2[...])
            dqt[...] += tn(kv[cc, 0], db[...])
            return carry

        lax.fori_loop(0, 2, one, 0)

    first_hop = {(0, 1): up, (0, -1): dn, (1, 1): dn, (1, -1): up}
    slots = {1: rp, -1: rm}

    def pass_on(i, way, hop):
        zz = at_z(way * hop)
        total = own[zz, i]
        if hop < first_hop[i, way]:
            slot = slots[way].at[i, hop]
            arrive(("kvg", i, way, hop + 1), slot)
            total = total + slot[...].astype(F32)
        snd[zz, i] = total.astype(BF16)
        send(("kvg", i, way, hop), snd.at[zz, i], slots[way].at[i, hop - 1], zdev(way))

    half = ntp // 2
    per_piece = DC // CW

    def weight_part(part, base, out):
        piece = base * half + part
        for head in range(2):
            rows = slice(head * HD, (head + 1) * HD)
            res = nn(att[head], gb[piece])
            for j in range(per_piece):
                out[part * per_piece + j, rows] = res[:, j * CW:(j + 1) * CW].astype(out.dtype)

    def weight_other():
        arrive("att", att.at[o])
        for part in range(half):
            weight_part(part, 1 - d, gws)
            block = pl.ds(part * per_piece, per_piece)
            send(("gw", part), gws.at[block], gwr.at[block], core)

    def weight_own():
        def one(part, carry):
            weight_part(part, d, gwo)
            return carry

        lax.fori_loop(0, half, one, 0)

    def weight_cross():
        for part in range(half):
            arrive(("gw", part), gwr.at[pl.ds(part * per_piece, per_piece)])
        for step in order:
            zz = at_z(step)
            gxs[zz] = (gwo[2 * zz + o] + gwr[2 * zz + o].astype(F32)).astype(BF16)
            send(("gwx", step), gxs.at[zz], gxr.at[zz], partner)

    order = [up] if nz > 1 else []
    for hop in range(dn, 0, -1):
        order += [hop, -hop]
    order += [0]
    gslots = {1: gp, -1: gm}
    tops = {1: pl.ds(0, F // 2), -1: pl.ds(F // 2, F // 2)}

    def weight_total(step):
        zz = at_z(step)
        arrive(("gwx", step), gxr.at[zz])
        gwo[2 * zz + h] = gwo[2 * zz + h] + gwr[2 * zz + h].astype(F32) + gxr[zz].astype(F32)

    def weight_add(zz, way, hop):
        rows = tops[way] if hop == up else pl.ds(0, F)
        slot = gslots[way].at[hop - 1, rows]
        arrive(("gwz", way, hop), slot)
        gwo[2 * zz + h, rows] = gwo[2 * zz + h, rows] + slot[...].astype(F32)

    def weight_far():
        weight_total(up)
        zz = at_z(up)
        gsn[zz] = gwo[2 * zz + h].astype(BF16)
        for way in (1, -1):
            send(("gwz", way, up), gsn.at[zz, tops[way]], gslots[way].at[up - 1, tops[way]], zdev(way))

    def weight_pass(way, hop):
        weight_total(way * hop)
        zz = at_z(way * hop)
        weight_add(zz, way, hop + 1)
        gsn[zz] = gwo[2 * zz + h].astype(BF16)
        send(("gwz", way, hop), gsn.at[zz], gslots[way].at[hop - 1], zdev(way))

    def gradient_pair(hop):
        gradients(hop)
        gradients(-hop)

    def finish(i):
        out = (dk_hbm, dv_hbm)[i]
        total = own[z, i]
        for way in (1, -1):
            if first_hop[i, way] > 0:
                arrive(("kvg", i, way, 1), slots[way].at[i, 0])
                total = total + slots[way][i, 0].astype(F32)
        fin[i] = total.astype(BF16)
        send(("fin", i), fin.at[i, o], out.at[0, :, hcols], partner)
        outs.append(local(i, fin.at[i, h], out.at[0, :, hcols]))

    outs = []

    def finish_q():
        dqb[...] = jnp.transpose(SCALE * dqt[...]).astype(BF16)
        send("dq", dqb.at[orows], dq_hbm.at[0, :, hcols], partner)
        outs.append(local(4, dqb.at[hrows], dq_hbm.at[0, :, hcols]))

    def finish_weight():
        weight_total(0)
        if nz > 1:
            weight_add(z, 1, 1)
            weight_add(z, -1, 1)
        gout[...] = gwo[2 * z + h].astype(BF16)
        outs.append(local(5, gout, gw_hbm))

    if nz > 1:
        gradients(up)
        pass_on(0, 1, up)
        pass_on(1, -1, up)
    if dn:
        gradient_pair(dn)
        pass_on(1, 1, dn)
        pass_on(0, -1, dn)
    work = [part(gradient_pair, hop) for hop in range(dn - 1, 0, -1)]
    work += [part(gradients, 0), finish_q]
    if work:
        work.pop(0)()
    weight_other()
    weight_own()
    if dn:
        pass_on(0, 1, dn)
        pass_on(1, -1, dn)
    while work:
        work.pop(0)()
    weight_cross()
    tasks = []
    for hop in range(dn - 1, 0, -1):
        tasks += [part(pass_on, 1, 1, hop), part(pass_on, 0, -1, hop)]
        tasks += [part(pass_on, 0, 1, hop), part(pass_on, 1, -1, hop)]
    tasks += [part(finish, 1), part(finish, 0)] if dn else [part(finish, 0), part(finish, 1)]
    more = [weight_far] if nz > 1 else []
    for hop in range(dn, 0, -1):
        more += [part(weight_pass, 1, hop), part(weight_pass, -1, hop)]
    for i, task in enumerate(tasks):
        task()
        if i >= 3 and more and i % 2 == 1:
            for task in more[:1 if more[0] is weight_far else 2]:
                task()
                more.pop(0)
    for task in more:
        task()
    finish_weight()

    arrive("dq", dq_hbm.at[0, :, ocols])
    arrive(("fin", 0), dk_hbm.at[0, :, ocols])
    arrive(("fin", 1), dv_hbm.at[0, :, ocols])
    for cp in outs:
        cp.wait()
    for cp in sent:
        cp.wait_send()
    assert len(sem.index) <= N_SEM


def hand_on(*refs):
    n = (len(refs) - 1) // 3
    ins, outs, bufs, sems = refs[:n], refs[n:2 * n], refs[2 * n:3 * n], refs[3 * n]
    reads = [pltpu.make_async_copy(a, b, sems.at[i]) for i, (a, b) in enumerate(zip(ins, bufs))]
    writes = [pltpu.make_async_copy(a, b, sems.at[n + i]) for i, (a, b) in enumerate(zip(bufs, outs))]
    for cp in reads:
        cp.start()
    for read, write in zip(reads, writes):
        read.wait()
        write.start()
    for cp in writes:
        cp.wait()


def per_device(nz, ny, q, k, v, g, w, pattern, offsets):
    T = q.shape[1]
    Q2 = 2 * T
    nctx, ntp = 2 * nz, 2 * ny
    DC, F = g.shape[2], w.shape[0]
    CW = w.shape[1] // (2 * nctx)
    deep = max(nz // 2, 1)
    V = pltpu.VMEM
    hbm = pl.BlockSpec(memory_space=pl.ANY)
    smem = pl.BlockSpec(memory_space=pltpu.SMEM)
    scratch = [
        V((nctx, 2, T, HD), BF16),
        V((Q2, HD), BF16),
        V((Q2, HD), BF16),
        V((ntp, T, DC), BF16),
        V(w.shape, BF16),
        V((T, F), F32),
        V((2, T, HD), BF16),
        V((nctx, T, 128), F32),
        V((nctx, 1, Q2), F32),
        V((nctx, T, Q2), F32),
        V((8, Q2), F32),
        V((8, Q2), F32),
        V((2 * deep + 4, 1, Q2), F32),
        V((HD, Q2), F32),
        V((HD, Q2), BF16),
        V((2, HD, T), BF16),
        V((T, Q2), BF16),
        V((T, Q2), BF16),
        V((nz, 2, 2, T, HD), F32),
        V((nz, 2, 2, T, HD), BF16),
        V((2, deep, 2, T, HD), BF16),
        V((2, deep, 2, T, HD), BF16),
        V((HD, Q2), F32),
        V((Q2, HD), BF16),
        V((2, 2, T, HD), BF16),
        V((nctx, F, CW), BF16),
        V((nctx, F, CW), BF16),
        V((nctx, F, CW), F32),
        V((nz, F, CW), BF16),
        V((nz, F, CW), BF16),
        V((nz, F, CW), BF16),
        V((deep, F, CW), BF16),
        V((deep, F, CW), BF16),
        V((F, CW), BF16),
        pltpu.SemaphoreType.DMA((N_SEM,)),
        pltpu.SemaphoreType.DMA((N_SEM,)),
        pltpu.SemaphoreType.DMA((6,)),
    ]
    like = jax.ShapeDtypeStruct(q.shape, BF16)
    shapes = (like, like, like, jax.ShapeDtypeStruct((F, CW), BF16))
    results = pl.pallas_call(
        functools.partial(kernel, nz, ny),
        out_shape=shapes,
        in_specs=[smem, smem, hbm, hbm, hbm, hbm, hbm],
        out_specs=(hbm, hbm, hbm, hbm),
        scratch_shapes=scratch,
        compiler_params=pltpu.CompilerParams(
            collective_id=0, has_side_effects=True, vmem_limit_bytes=60 * 1024 * 1024
        ),
        name="attention_backward",
    )(pattern.T, offsets.T, q, k, v, g, w)
    return tuple(
        pl.pallas_call(
            hand_on,
            out_shape=shapes,
            in_specs=[hbm] * 4,
            out_specs=(hbm,) * 4,
            scratch_shapes=[V(s.shape, BF16) for s in shapes] + [pltpu.SemaphoreType.DMA((8,))],
            name="hand_on",
        )(*results)
    )


def solution(mesh):
    nz, ny = mesh.shape["ctx"] // 2, mesh.shape["tp"] // 2
    spec = P("dp", "ctx", "tp")
    return jax.shard_map(
        functools.partial(per_device, nz, ny),
        mesh=mesh,
        in_specs=(spec, spec, spec, spec, P("tp", None), P(), P()),
        out_specs=(spec, spec, spec, P("tp", ("dp", "ctx"))),
        check_vma=False,
    )
```

```python
import functools

import jax
import jax.numpy as jnp
from jax import lax
from jax.experimental import pallas as pl
from jax.experimental.pallas import tpu as pltpu
from jax.sharding import PartitionSpec as P

HD = 128
LOWEST = -1e30
SCALE = HD ** (-0.5)
LOG2E = 1.4426950408889634
MESH = pl.DeviceIdType.MESH
F32 = jnp.float32
BF16 = jnp.bfloat16


def nt(a, b):
    return lax.dot_general(a, b, (((1,), (1,)), ((), ())), preferred_element_type=F32)


def tn(a, b):
    return lax.dot_general(a, b, (((0,), (0,)), ((), ())), preferred_element_type=F32)


def nn(a, b):
    return jnp.dot(a, b, preferred_element_type=F32)


def any_of(flags):
    return functools.reduce(jnp.logical_or, flags)


class Sems:
    def __init__(self):
        self.index = {}

    def __getitem__(self, name):
        return self.index.setdefault(name, len(self.index))


N_SEM = 160
EARLY = 1


def arrival_times(flows):
    done, free = {}, {}
    left = dict(flows)
    while left:
        ready = []
        for name, (needs, delay, link, busy, wait) in left.items():
            if all(n in done for n in needs):
                start = max([done[n] for n in needs] + [0.0]) + delay
                ready.append((start, len(ready), name))
        start, _, name = min(ready)
        _, _, link, busy, wait = left.pop(name)
        begin = max(start, free.get(link, 0.0))
        free[link] = begin + busy
        done[name] = begin + busy + wait
    return done


def kernel(
    nz,
    ny,
    pat,
    offs,
    q_hbm,
    k_hbm,
    v_hbm,
    g_hbm,
    w_hbm,
    dq_hbm,
    dk_hbm,
    dv_hbm,
    gw_hbm,
    kv,
    q2,
    do2,
    gb,
    wv,
    gh,
    ghb,
    kb,
    qb,
    sb,
    mx,
    lr,
    stat,
    ot,
    ob,
    att,
    pb,
    db,
    own,
    snd,
    rp,
    rm,
    dqt,
    dqb,
    fin,
    gws,
    gwr,
    gwo,
    gxs,
    gxr,
    gsn,
    gp,
    gm,
    gout,
    ss,
    rs,
    ls,
    here,
):
    T = q_hbm.shape[1]
    Q2 = 2 * T
    nctx, ntp = 2 * nz, 2 * ny
    DC = g_hbm.shape[2]
    F = w_hbm.shape[0]
    CW = gw_hbm.shape[1]
    GB = offs.shape[0]
    up, dn = nz // 2, max(nz // 2 - 1, 0)
    yup, ydn = ny // 2, max(ny // 2 - 1, 0)
    lanes = [slice(i * 128, (i + 1) * 128) for i in range(Q2 // 128)]

    d = lax.axis_index("dp")
    c = lax.axis_index("ctx")
    t = lax.axis_index("tp")
    z, h = lax.div(c, 2), lax.rem(c, 2)
    y, xl = lax.div(t, 2), lax.rem(t, 2)
    o = 1 - h

    def at_z(step):
        return lax.rem(z + (step + nz), nz)

    def at_y(step):
        return lax.rem(y + (step + ny), ny)

    def zdev(step, column=None):
        return (d, at_z(step) * 2 + (h if column is None else column), t)

    def ydev(step):
        return (d, c, at_y(step) * 2 + xl)

    partner = (d, 2 * z + o, t)
    xdev = (d, c, 2 * y + 1 - xl)
    core = (1 - d, c, t)
    hcols = pl.ds(pl.multiple_of(h * HD, HD), HD)
    ocols = pl.ds(pl.multiple_of(o * HD, HD), HD)
    hrows = pl.ds(pl.multiple_of(h * T, T), T)
    orows = pl.ds(pl.multiple_of(o * T, T), T)

    sem = Sems()
    sent = []

    def send(name, src, dst, dev):
        i = sem[name]
        cp = pltpu.make_async_remote_copy(
            src_ref=src, dst_ref=dst, send_sem=ss.at[i], recv_sem=rs.at[i],
            device_id=dev, device_id_type=MESH,
        )
        cp.start()
        sent.append(cp)

    def arrive(name, dst):
        i = sem[name]
        pltpu.make_async_remote_copy(
            src_ref=dst, dst_ref=dst, send_sem=ss.at[i], recv_sem=rs.at[i],
            device_id=partner, device_id_type=MESH,
        ).wait_recv()

    def local(i, src, dst):
        cp = pltpu.make_async_copy(src, dst, ls.at[i])
        cp.start()
        return cp

    load_k = local(0, k_hbm.at[0, :, hcols], kv.at[c, 0])
    load_v = local(1, v_hbm.at[0, :, hcols], kv.at[c, 1])
    load_q = local(2, q_hbm.at[0, :, hcols], q2.at[hrows])
    load_g = local(3, g_hbm.at[0], gb.at[t])
    load_w = local(4, w_hbm, wv)

    near = [partner, xdev]
    if nz > 1:
        near += [zdev(1), zdev(-1)]
    if ny > 1:
        near += [ydev(1), ydev(-1)]
    barrier = pltpu.get_barrier_semaphore()
    for dev in near:
        pl.semaphore_signal(barrier, inc=1, device_id=dev, device_id_type=MESH)

    @pl.when(d == 0)
    def _():
        pl.semaphore_signal(barrier, inc=1, device_id=core, device_id_type=MESH)

    pl.semaphore_wait(barrier, len(near) + d)

    @pl.when(d == 1)
    def _():
        pl.semaphore_signal(here, inc=1, device_id=core, device_id_type=MESH)


    halves = [pl.ds(i * (T // 2), T // 2) for i in range(2)]

    hops = {("a", 1): up, ("a", -1): dn, ("b", 1): dn, ("b", -1): up}

    def z_block(chain, step):
        return 2 * at_z(step) + (h if chain == "a" else o)

    def z_send(chain, way, hop, i, j):
        if hop < hops[chain, way]:
            block = kv.at[z_block(chain, -way * hop), i, halves[j]]
            send(("kv", chain, way, hop + 1, i, j), block, block, zdev(way))

    def y_piece(chain, step):
        return 2 * at_y(step) + (xl if chain == "a" else 1 - xl)

    def y_goes(chain, way, hop, i):
        if hop < yup:
            return True
        return hop == yup and chain == "a" and i == (0 if way == 1 else 1)

    def y_send(chain, way, hop, i):
        if y_goes(chain, way, hop + 1, i):
            piece = gb.at[y_piece(chain, -way * hop), halves[i]]
            src = g_hbm.at[0, halves[i]] if chain == "a" and hop == 0 else piece
            send(("g", chain, way, hop + 1, i), src, piece, ydev(way))

    def x_send(i):
        send(("gx", i), g_hbm.at[0, halves[i]], gb.at[t, halves[i]], xdev)

    for i, src in ((0, k_hbm), (1, v_hbm)):
        for j in range(2):
            send(("kv"[i], j), src.at[0, halves[j], ocols], kv.at[c, i, halves[j]], partner)
    for i in range(2):
        y_send("a", 1, 0, i)
        y_send("a", -1, 0, 1 - i)
    x_send(0)
    x_send(1)
    send("q", q_hbm.at[0, :, ocols], q2.at[hrows], partner)
    for i, load in ((0, load_k), (1, load_v)):
        load.wait()
        for j in range(2):
            z_send("a", 1, 0, i, j)
            z_send("a", -1, 0, i, j)

    lane = lax.broadcasted_iota(jnp.int32, (1, Q2), 1)
    is_first = lane < T
    pos = jnp.where(is_first, lane, lane - T)
    b0 = 2 * z
    bvec = jnp.where(is_first, b0, b0 + 1)

    def both(ref, k):
        return jnp.where(is_first, ref[k, b0], ref[k, b0 + 1])

    row_global = any_of([pos == both(offs, g) for g in range(GB)])
    picks = [both(pat, r) for r in range(pat.shape[0])]
    for cc in range(nctx):
        seen = any_of([row_global, jnp.abs(bvec - cc) <= 1] + [pick == cc for pick in picks])
        qb[cc] = jnp.where(seen, 0.0, LOWEST)

    def key_bias(cc, carry):
        row = lax.broadcasted_iota(jnp.int32, (T, 128), 0)
        kb[cc] = jnp.where(any_of([row == offs[g, cc] for g in range(GB)]), 0.0, LOWEST)
        return carry

    lax.fori_loop(0, nctx, key_bias, 0)
    mx[...] = jnp.full_like(mx, LOWEST)
    gh[...] = jnp.zeros_like(gh)
    lr[...] = jnp.zeros_like(lr)
    ot[...] = jnp.zeros_like(ot)

    def score(cc):
        s = nt(kv[cc, 0], q2[...])
        bias = kb[cc]
        row_bias = qb[cc]
        for sl in lanes:
            part = s[:, sl] + jnp.maximum(bias, row_bias[:, sl])
            sb[cc, :, sl] = part
            mx[:, sl] = jnp.maximum(mx[:, sl], jnp.max(part.reshape(T // 8, 8, 128), axis=0))

    def project(tt):
        cols = pl.ds(pl.multiple_of(tt * DC, DC), DC)
        gh[...] += nt(gb[tt], wv[:, cols])

    group_of = {step: max(abs(step) - 1, 0) for step in range(-dn, up + 1)}
    n_group = max(group_of.values()) + 1
    TOTAL, DOT, FACTOR = n_group, n_group + 1, n_group + 2

    def weigh(j):
        stat[j] = jnp.max(mx[...], axis=0, keepdims=True)
        if j:
            scale = jnp.exp2((stat[j - 1] - stat[j]) * (SCALE * LOG2E))
            ot[...] = ot[...] * scale
            lr[...] = lr[...] * scale

        def one(cc):
            for sl in lanes:
                e = jnp.exp2((sb[cc, :, sl] - stat[j, :, sl]) * (SCALE * LOG2E))
                sb[cc, :, sl] = e
                lr[:, sl] += jnp.sum(e.reshape(T // 8, 8, 128), axis=0)
                pb[:, sl] = e.astype(BF16)
            ot[...] += tn(kv[cc, 1], pb[...])

        for step in [step for step, group in group_of.items() if group == j]:

            def pair(x, carry, step=step):
                one(2 * at_z(step) + x)
                return carry

            lax.fori_loop(0, 2, pair, 0)

    ready = {"q": False, "blocks": []}
    missing = {j: sum(8 for group in group_of.values() if group == j) for j in range(n_group)}

    def landed(step, count=1):
        missing[group_of[step]] -= count
        while missing and ready["q"] and missing[min(missing)] == 0:
            j = min(missing)
            del missing[j]
            weigh(j)

    def scores_of(cc):
        if ready["q"]:
            score(cc)
        else:
            ready["blocks"].append(cc)

    def on_own():
        load_g.wait()
        load_w.wait()
        project(t)
        scores_of(z_block("a", 0))
        landed(0, 4)

    def on_q():
        load_q.wait()
        arrive("q", q2.at[orows])
        ready["q"] = True
        for cc in ready["blocks"]:
            score(cc)
        landed(0, 0)

    def on_pair(i, j):
        pair = z_block("b", 0)
        arrive(("kv"[i], j), kv.at[pair, i, halves[j]])
        z_send("b", 1, 0, i, j)
        z_send("b", -1, 0, i, j)
        if i == 0 and j == 1:
            scores_of(pair)
        landed(0)

    def on_gx(i):
        piece = y_piece("b", 0)
        arrive(("gx", i), gb.at[piece, halves[i]])
        y_send("b", 1, 0, i)
        y_send("b", -1, 0, i)
        if i:
            project(piece)

    def on_kv(chain, way, hop, i, j):
        step = -way * hop
        if step == -up:
            step = up
        block = z_block(chain, step)
        arrive(("kv", chain, way, hop, i, j), kv.at[block, i, halves[j]])
        z_send(chain, way, hop, i, j)
        if i == 0 and j == 1:
            scores_of(block)
        landed(step)

    pieces = {}

    def piece_half(chain, step):
        step = yup if step == -yup else step
        pieces[chain, step] = pieces.get((chain, step), 0) + 1
        if pieces[chain, step] == 2:
            project(y_piece(chain, step))

    def on_g(chain, way, hop, i):
        step = yup if hop == yup else -way * hop
        here = gb.at[y_piece(chain, step), halves[i]]
        arrive(("g", chain, way, hop, i), here)
        y_send(chain, way, hop, i)
        if hop == yup:
            send(("gc", i), here, here, xdev)
        piece_half(chain, step)

    def on_gc(i):
        arrive(("gc", i), gb.at[y_piece("b", yup), halves[i]])
        piece_half("b", yup)

    us = 2.0 / 88e3
    kv_us, g_us = T * HD * 2 * us, T * DC * us
    part = functools.partial
    flows, events = {}, {}

    def flow(name, needs, delay, link, busy, wait, event):
        flows[name] = (needs, delay, link, busy, wait)
        events[name] = event

    for i in range(2):
        for j in range(2):
            flow(("kv"[i], j), (), 0, "x", kv_us / 2, 2.6, part(on_pair, i, j))
    for i in range(2):
        flow(("gx", i), (), 0, "x", g_us, 1.8, part(on_gx, i))
    flow("q", (), 0, "x", kv_us, 2.6, on_q)
    for i in range(2):
        for (chain, way), count in hops.items():
            for hop, j in [(hop, j) for hop in range(1, count + 1) for j in range(2)]:
                first = () if chain == "a" else (("kv"[i], j),)
                needs = (("kv", chain, way, hop - 1, i, j),) if hop > 1 else first
                name = ("kv", chain, way, hop, i, j)
                flow(name, needs, 0.1, ("z", way), kv_us / 2, 2.2, part(on_kv, chain, way, hop, i, j))
        for chain in "ab":
            for way in (1, -1):
                for hop in range(1, yup + 1):
                    if y_goes(chain, way, hop, i):
                        first = () if chain == "a" else (("gx", i),)
                        needs = (("g", chain, way, hop - 1, i),) if hop > 1 else first
                        late = 0.2 if i == (0 if way == -1 else 1) else 0.1
                        name = ("g", chain, way, hop, i)
                        flow(name, needs, late, ("y", way), g_us, 1.8, part(on_g, chain, way, hop, i))
                        if hop == yup:
                            flow(("gc", i), (name,), 0.1, "x", g_us, 1.8, part(on_gc, i))
    times = arrival_times(flows)

    def gather(names):
        for name in sorted(names, key=times.get):
            events[name]()

    last_g = max([times[name] for name in events if name[0] in ("g", "gx", "gc")])
    on_own()
    gather([name for name in events if times[name] <= last_g])
    ghb[0] = gh[:, :HD].astype(BF16)
    ghb[1] = gh[:, HD:].astype(BF16)
    send("do", ghb.at[o], do2.at[hrows], partner)
    do2[hrows, :] = ghb[h]
    gather([name for name in events if times[name] > last_g])

    inverse = 1.0 / jnp.sum(lr[...], axis=0, keepdims=True)
    low = (ot[...] * inverse).astype(BF16)
    ob[...] = low
    send("att", ob.at[:, orows], att.at[h], partner)
    att[h] = ob[:, hrows]
    for j in range(n_group):
        back = jnp.exp2((stat[j] - stat[n_group - 1]) * (SCALE * LOG2E))
        stat[FACTOR + j] = inverse * back
    arrive("do", do2.at[orows])
    do_t = jnp.transpose(do2[...].astype(F32))
    stat[DOT] = jnp.sum(do_t * low.astype(F32), axis=0, keepdims=True)
    dqt[...] = jnp.zeros_like(dqt)

    def gradients(step):
        zz = at_z(step)
        factor = stat.at[FACTOR + group_of[step]]

        def one(x, carry):
            cc = 2 * zz + x
            dp = nt(kv[cc, 1], do2[...])
            for sl in lanes:
                p = sb[cc, :, sl] * factor[:, sl]
                pb[:, sl] = p.astype(BF16)
                db[:, sl] = (p * (dp[:, sl] - stat[DOT, :, sl])).astype(BF16)
            own[zz, 0, x] = SCALE * nn(db[...], q2[...])
            own[zz, 1, x] = nn(pb[...], do2[...])
            dqt[...] += tn(kv[cc, 0], db[...])
            return carry

        lax.fori_loop(0, 2, one, 0)

    first_hop = {(0, 1): up, (0, -1): dn, (1, 1): dn, (1, -1): up}
    slots = {1: rp, -1: rm}

    def pass_on(i, way, hop):
        zz = at_z(way * hop)
        for x in (o, h):
            total = own[zz, i, x]
            if hop < first_hop[i, way]:
                slot = slots[way].at[i, hop, x]
                arrive(("kvg", i, way, hop + 1, x is o), slot)
                total = total + slot[...].astype(F32)
            snd[zz, i, x] = total.astype(BF16)
            send(("kvg", i, way, hop, x is o), snd.at[zz, i, x], slots[way].at[i, hop - 1, x], zdev(way))

    half = ntp // 2
    per_piece = DC // CW

    def weight_part(head, part, base, out):
        piece = base * half + part
        rows = pl.ds(pl.multiple_of(head * HD, HD), HD)
        res = nn(att[head], gb[piece])
        for j in range(per_piece):
            out[part * per_piece + j, rows] = res[:, j * CW:(j + 1) * CW].astype(out.dtype)

    def weight_other(phase):
        head = o if phase else h
        rows = pl.ds(pl.multiple_of(head * HD, HD), HD)
        if phase:
            arrive("att", att.at[o])
        else:

            @pl.when(d == 0)
            def _():
                pl.semaphore_wait(here, 1)

        for part in range(half):
            weight_part(head, part, 1 - d, gws)
            block = pl.ds(part * per_piece, per_piece)
            send(("gw", phase, part), gws.at[block, rows], gwr.at[block, rows], core)

    def weight_own(phase):
        def one(part, carry):
            weight_part(o if phase else h, part, d, gwo)
            return carry

        lax.fori_loop(0, half, one, 0)

    def weight_cross(phase):
        head = o if phase else h
        rows = pl.ds(pl.multiple_of(head * HD, HD), HD)
        for part in range(half):
            arrive(("gw", phase, part), gwr.at[pl.ds(part * per_piece, per_piece), rows])
        for step in order:
            zz = at_z(step)
            gxs[zz, rows] = (gwo[2 * zz + o, rows] + gwr[2 * zz + o, rows].astype(F32)).astype(BF16)
            send(("gwx", phase, step), gxs.at[zz, rows], gxr.at[zz, rows], partner)

    order = [up] if nz > 1 else []
    for hop in range(dn, 0, -1):
        order += [hop, -hop]
    order += [0]
    gslots = {1: gp, -1: gm}
    tops = {1: pl.ds(0, F // 2), -1: pl.ds(F // 2, F // 2)}

    def weight_total(step):
        zz = at_z(step)
        for phase in range(2):
            head = h if phase else o
            rows = pl.ds(pl.multiple_of(head * HD, HD), HD)
            arrive(("gwx", phase, step), gxr.at[zz, rows])
        gwo[2 * zz + h] = gwo[2 * zz + h] + gwr[2 * zz + h].astype(F32) + gxr[zz].astype(F32)

    def weight_add(zz, way, hop):
        rows = tops[way] if hop == up else pl.ds(0, F)
        slot = gslots[way].at[hop - 1, rows]
        arrive(("gwz", way, hop), slot)
        gwo[2 * zz + h, rows] = gwo[2 * zz + h, rows] + slot[...].astype(F32)

    def weight_far():
        weight_total(up)
        zz = at_z(up)
        gsn[zz] = gwo[2 * zz + h].astype(BF16)
        for way in (1, -1):
            send(("gwz", way, up), gsn.at[zz, tops[way]], gslots[way].at[up - 1, tops[way]], zdev(way))

    def weight_pass(way, hop):
        weight_total(way * hop)
        zz = at_z(way * hop)
        weight_add(zz, way, hop + 1)
        gsn[zz] = gwo[2 * zz + h].astype(BF16)
        send(("gwz", way, hop), gsn.at[zz], gslots[way].at[hop - 1], zdev(way))

    def gradient_pair(hop):
        gradients(hop)
        gradients(-hop)

    def finish(i, x):
        out = (dk_hbm, dv_hbm)[i]
        total = own[z, i, x]
        for way in (1, -1):
            if first_hop[i, way] > 0:
                arrive(("kvg", i, way, 1, x is o), slots[way].at[i, 0, x])
                total = total + slots[way][i, 0, x].astype(F32)
        fin[i, x] = total.astype(BF16)
        if x is o:
            send(("fin", i), fin.at[i, o], out.at[0, :, hcols], partner)
        else:
            outs.append(local(i, fin.at[i, h], out.at[0, :, hcols]))

    outs = []

    def finish_q():
        dqb[...] = jnp.transpose(SCALE * dqt[...]).astype(BF16)
        send("dq", dqb.at[orows], dq_hbm.at[0, :, hcols], partner)
        outs.append(local(4, dqb.at[hrows], dq_hbm.at[0, :, hcols]))

    def finish_weight():
        weight_total(0)
        if nz > 1:
            weight_add(z, 1, 1)
            weight_add(z, -1, 1)
        gout[...] = gwo[2 * z + h].astype(BF16)
        outs.append(local(5, gout, gw_hbm))

    if nz > 1:
        gradients(up)
        pass_on(0, 1, up)
        pass_on(1, -1, up)
    weight_other(0)
    if dn:
        gradient_pair(dn)
        pass_on(1, 1, dn)
        pass_on(0, -1, dn)
    weight_own(0)
    work = [part(gradient_pair, hop) for hop in range(dn - 1, 0, -1)]
    work += [part(gradients, 0), finish_q]
    weight_cross(0)
    weight_other(1)
    if dn:
        pass_on(0, 1, dn)
        pass_on(1, -1, dn)
    work.pop(0)()
    weight_own(1)
    weight_cross(1)
    tasks = []
    for hop in range(dn - 1, 0, -1):
        tasks += [part(pass_on, 1, 1, hop), part(pass_on, 0, -1, hop)]
        tasks += [part(pass_on, 0, 1, hop), part(pass_on, 1, -1, hop)]
    ends = (1, 0) if dn else (0, 1)
    more = [weight_far] if nz > 1 else []
    for hop in range(dn, 0, -1):
        more += [part(weight_pass, 1, hop), part(weight_pass, -1, hop)]
    for i, task in enumerate(tasks):
        task()
        if i == 1:
            while work:
                work.pop(0)()
        if i % 2 == 1 and i >= EARLY and more:
            for task in more[:1 if more[0] is weight_far else 2]:
                task()
                more.pop(0)
    while work:
        work.pop(0)()
    for i in ends:
        finish(i, o)
    for task in more[:-2]:
        task()
    for i in ends:
        finish(i, h)
    for task in more[-2:]:
        task()
    finish_weight()

    arrive("dq", dq_hbm.at[0, :, ocols])
    arrive(("fin", 0), dk_hbm.at[0, :, ocols])
    arrive(("fin", 1), dv_hbm.at[0, :, ocols])
    for cp in outs:
        cp.wait()
    for cp in sent:
        cp.wait_send()
    assert len(sem.index) <= N_SEM


def hand_on(*refs):
    n = (len(refs) - 1) // 3
    ins, outs, bufs, sems = refs[:n], refs[n:2 * n], refs[2 * n:3 * n], refs[3 * n]
    reads = [pltpu.make_async_copy(a, b, sems.at[i]) for i, (a, b) in enumerate(zip(ins, bufs))]
    writes = [pltpu.make_async_copy(a, b, sems.at[n + i]) for i, (a, b) in enumerate(zip(bufs, outs))]
    for cp in reads:
        cp.start()
    for read, write in zip(reads, writes):
        read.wait()
        write.start()
    for cp in writes:
        cp.wait()


def per_device(nz, ny, q, k, v, g, w, pattern, offsets):
    T = q.shape[1]
    Q2 = 2 * T
    nctx, ntp = 2 * nz, 2 * ny
    DC, F = g.shape[2], w.shape[0]
    CW = w.shape[1] // (2 * nctx)
    deep = max(nz // 2, 1)
    V = pltpu.VMEM
    hbm = pl.BlockSpec(memory_space=pl.ANY)
    smem = pl.BlockSpec(memory_space=pltpu.SMEM)
    scratch = [
        V((nctx, 2, T, HD), BF16),
        V((Q2, HD), BF16),
        V((Q2, HD), BF16),
        V((ntp, T, DC), BF16),
        V(w.shape, BF16),
        V((T, F), F32),
        V((2, T, HD), BF16),
        V((nctx, T, 128), F32),
        V((nctx, 1, Q2), F32),
        V((nctx, T, Q2), F32),
        V((8, Q2), F32),
        V((8, Q2), F32),
        V((2 * deep + 4, 1, Q2), F32),
        V((HD, Q2), F32),
        V((HD, Q2), BF16),
        V((2, HD, T), BF16),
        V((T, Q2), BF16),
        V((T, Q2), BF16),
        V((nz, 2, 2, T, HD), F32),
        V((nz, 2, 2, T, HD), BF16),
        V((2, deep, 2, T, HD), BF16),
        V((2, deep, 2, T, HD), BF16),
        V((HD, Q2), F32),
        V((Q2, HD), BF16),
        V((2, 2, T, HD), BF16),
        V((nctx, F, CW), BF16),
        V((nctx, F, CW), BF16),
        V((nctx, F, CW), F32),
        V((nz, F, CW), BF16),
        V((nz, F, CW), BF16),
        V((nz, F, CW), BF16),
        V((deep, F, CW), BF16),
        V((deep, F, CW), BF16),
        V((F, CW), BF16),
        pltpu.SemaphoreType.DMA((N_SEM,)),
        pltpu.SemaphoreType.DMA((N_SEM,)),
        pltpu.SemaphoreType.DMA((6,)),
        pltpu.SemaphoreType.REGULAR,
    ]
    like = jax.ShapeDtypeStruct(q.shape, BF16)
    shapes = (like, like, like, jax.ShapeDtypeStruct((F, CW), BF16))
    results = pl.pallas_call(
        functools.partial(kernel, nz, ny),
        out_shape=shapes,
        in_specs=[smem, smem, hbm, hbm, hbm, hbm, hbm],
        out_specs=(hbm, hbm, hbm, hbm),
        scratch_shapes=scratch,
        compiler_params=pltpu.CompilerParams(
            collective_id=0, has_side_effects=True, vmem_limit_bytes=60 * 1024 * 1024
        ),
        name="attention_backward",
    )(pattern.T, offsets.T, q, k, v, g, w)
    return tuple(
        pl.pallas_call(
            hand_on,
            out_shape=shapes,
            in_specs=[hbm] * 4,
            out_specs=(hbm,) * 4,
            scratch_shapes=[V(s.shape, BF16) for s in shapes] + [pltpu.SemaphoreType.DMA((8,))],
            name="hand_on",
        )(*results)
    )


def solution(mesh):
    nz, ny = mesh.shape["ctx"] // 2, mesh.shape["tp"] // 2
    spec = P("dp", "ctx", "tp")
    return jax.shard_map(
        functools.partial(per_device, nz, ny),
        mesh=mesh,
        in_specs=(spec, spec, spec, spec, P("tp", None), P(), P()),
        out_specs=(spec, spec, spec, P("tp", ("dp", "ctx"))),
        check_vma=False,
    )
```

```python
import functools

import jax
import jax.numpy as jnp
from jax import lax
from jax.experimental import pallas as pl
from jax.experimental.pallas import tpu as pltpu
from jax.sharding import PartitionSpec as P

HD = 128
LOWEST = -1e30
SCALE = HD ** (-0.5)
LOG2E = 1.4426950408889634
MESH = pl.DeviceIdType.MESH
F32 = jnp.float32
BF16 = jnp.bfloat16


def nt(a, b):
    return lax.dot_general(a, b, (((1,), (1,)), ((), ())), preferred_element_type=F32)


def tn(a, b):
    return lax.dot_general(a, b, (((0,), (0,)), ((), ())), preferred_element_type=F32)


def nn(a, b):
    return jnp.dot(a, b, preferred_element_type=F32)


def any_of(flags):
    return functools.reduce(jnp.logical_or, flags)


class Sems:
    def __init__(self):
        self.index = {}

    def __getitem__(self, name):
        return self.index.setdefault(name, len(self.index))


N_SEM = 160
EARLY = 1


def arrival_times(flows):
    done, free = {}, {}
    left = dict(flows)
    while left:
        ready = []
        for name, (needs, delay, link, busy, wait) in left.items():
            if all(n in done for n in needs):
                start = max([done[n] for n in needs] + [0.0]) + delay
                ready.append((start, len(ready), name))
        start, _, name = min(ready)
        _, _, link, busy, wait = left.pop(name)
        begin = max(start, free.get(link, 0.0))
        free[link] = begin + busy
        done[name] = begin + busy + wait
    return done


def kernel(
    nz,
    ny,
    pat,
    offs,
    q_hbm,
    k_hbm,
    v_hbm,
    g_hbm,
    w_hbm,
    dq_hbm,
    dk_hbm,
    dv_hbm,
    gw_hbm,
    kv,
    q2,
    do2,
    gb,
    wv,
    gh,
    ghb,
    kb,
    qb,
    sb,
    mx,
    lr,
    stat,
    ot,
    ob,
    att,
    pb,
    db,
    own,
    snd,
    rp,
    rm,
    dqt,
    dqb,
    fin,
    gws,
    gwr,
    gwo,
    gxs,
    gxr,
    gsn,
    gp,
    gm,
    gout,
    ss,
    rs,
    ls,
    here,
):
    T = q_hbm.shape[1]
    Q2 = 2 * T
    nctx, ntp = 2 * nz, 2 * ny
    DC = g_hbm.shape[2]
    F = w_hbm.shape[0]
    CW = gw_hbm.shape[1]
    GB = offs.shape[0]
    up, dn = nz // 2, max(nz // 2 - 1, 0)
    yup, ydn = ny // 2, max(ny // 2 - 1, 0)
    lanes = [slice(i * 128, (i + 1) * 128) for i in range(Q2 // 128)]

    d = lax.axis_index("dp")
    c = lax.axis_index("ctx")
    t = lax.axis_index("tp")
    z, h = lax.div(c, 2), lax.rem(c, 2)
    y, xl = lax.div(t, 2), lax.rem(t, 2)
    o = 1 - h

    def at_z(step):
        return lax.rem(z + (step + nz), nz)

    def at_y(step):
        return lax.rem(y + (step + ny), ny)

    def zdev(step, column=None):
        return (d, at_z(step) * 2 + (h if column is None else column), t)

    def ydev(step):
        return (d, c, at_y(step) * 2 + xl)

    partner = (d, 2 * z + o, t)
    xdev = (d, c, 2 * y + 1 - xl)
    core = (1 - d, c, t)
    hcols = pl.ds(pl.multiple_of(h * HD, HD), HD)
    ocols = pl.ds(pl.multiple_of(o * HD, HD), HD)
    hrows = pl.ds(pl.multiple_of(h * T, T), T)
    orows = pl.ds(pl.multiple_of(o * T, T), T)

    sem = Sems()
    sent = []

    def send(name, src, dst, dev):
        i = sem[name]
        cp = pltpu.make_async_remote_copy(
            src_ref=src, dst_ref=dst, send_sem=ss.at[i], recv_sem=rs.at[i],
            device_id=dev, device_id_type=MESH,
        )
        cp.start()
        sent.append(cp)

    def arrive(name, dst):
        i = sem[name]
        pltpu.make_async_remote_copy(
            src_ref=dst, dst_ref=dst, send_sem=ss.at[i], recv_sem=rs.at[i],
            device_id=partner, device_id_type=MESH,
        ).wait_recv()

    def local(i, src, dst):
        cp = pltpu.make_async_copy(src, dst, ls.at[i])
        cp.start()
        return cp

    load_k = local(0, k_hbm.at[0, :, hcols], kv.at[c, 0])
    load_v = local(1, v_hbm.at[0, :, hcols], kv.at[c, 1])
    load_q = local(2, q_hbm.at[0, :, hcols], q2.at[hrows])
    load_g = local(3, g_hbm.at[0], gb.at[t])
    load_w = local(4, w_hbm, wv)

    near = [partner, xdev]
    if nz > 1:
        near += [zdev(1), zdev(-1)]
    if ny > 1:
        near += [ydev(1), ydev(-1)]
    barrier = pltpu.get_barrier_semaphore()
    for dev in near:
        pl.semaphore_signal(barrier, inc=1, device_id=dev, device_id_type=MESH)

    @pl.when(d == 0)
    def _():
        pl.semaphore_signal(barrier, inc=1, device_id=core, device_id_type=MESH)

    pl.semaphore_wait(barrier, len(near) + d)

    @pl.when(d == 1)
    def _():
        pl.semaphore_signal(here, inc=1, device_id=core, device_id_type=MESH)


    halves = [pl.ds(i * (T // 2), T // 2) for i in range(2)]

    hops = {("a", 1): up, ("a", -1): dn, ("b", 1): dn, ("b", -1): up}

    def z_block(chain, step):
        return 2 * at_z(step) + (h if chain == "a" else o)

    def z_send(chain, way, hop, i, j):
        if hop < hops[chain, way]:
            block = kv.at[z_block(chain, -way * hop), i, halves[j]]
            send(("kv", chain, way, hop + 1, i, j), block, block, zdev(way))

    def y_piece(chain, step):
        return 2 * at_y(step) + (xl if chain == "a" else 1 - xl)

    def y_goes(chain, way, hop, i):
        if hop < yup:
            return True
        return hop == yup and chain == "a" and i == (0 if way == 1 else 1)

    def y_send(chain, way, hop, i):
        if y_goes(chain, way, hop + 1, i):
            piece = gb.at[y_piece(chain, -way * hop), halves[i]]
            src = g_hbm.at[0, halves[i]] if chain == "a" and hop == 0 else piece
            send(("g", chain, way, hop + 1, i), src, piece, ydev(way))

    def x_send(i):
        send(("gx", i), g_hbm.at[0, halves[i]], gb.at[t, halves[i]], xdev)

    for i, src in ((0, k_hbm), (1, v_hbm)):
        for j in range(2):
            send(("kv"[i], j), src.at[0, halves[j], ocols], kv.at[c, i, halves[j]], partner)
    for i in range(2):
        y_send("a", 1, 0, i)
        y_send("a", -1, 0, 1 - i)
    x_send(0)
    x_send(1)
    send("q", q_hbm.at[0, :, ocols], q2.at[hrows], partner)
    for i, load in ((0, load_k), (1, load_v)):
        load.wait()
        for j in range(2):
            z_send("a", 1, 0, i, j)
            z_send("a", -1, 0, i, j)

    lane = lax.broadcasted_iota(jnp.int32, (1, Q2), 1)
    is_first = lane < T
    pos = jnp.where(is_first, lane, lane - T)
    b0 = 2 * z
    bvec = jnp.where(is_first, b0, b0 + 1)

    def both(ref, k):
        return jnp.where(is_first, ref[k, b0], ref[k, b0 + 1])

    row_global = any_of([pos == both(offs, g) for g in range(GB)])
    picks = [both(pat, r) for r in range(pat.shape[0])]
    for cc in range(nctx):
        seen = any_of([row_global, jnp.abs(bvec - cc) <= 1] + [pick == cc for pick in picks])
        qb[cc] = jnp.where(seen, 0.0, LOWEST)

    def key_bias(cc, carry):
        row = lax.broadcasted_iota(jnp.int32, (T, 128), 0)
        kb[cc] = jnp.where(any_of([row == offs[g, cc] for g in range(GB)]), 0.0, LOWEST)
        return carry

    lax.fori_loop(0, nctx, key_bias, 0)
    mx[...] = jnp.full_like(mx, LOWEST)
    gh[...] = jnp.zeros_like(gh)
    lr[...] = jnp.zeros_like(lr)
    ot[...] = jnp.zeros_like(ot)

    def score(cc):
        s = nt(kv[cc, 0], q2[...])
        bias = kb[cc]
        row_bias = qb[cc]
        for sl in lanes:
            part = s[:, sl] + jnp.maximum(bias, row_bias[:, sl])
            sb[cc, :, sl] = part
            mx[:, sl] = jnp.maximum(mx[:, sl], jnp.max(part.reshape(T // 8, 8, 128), axis=0))

    def project(tt):
        cols = pl.ds(pl.multiple_of(tt * DC, DC), DC)
        gh[...] += nt(gb[tt], wv[:, cols])

    group_of = {step: max(abs(step) - 1, 0) for step in range(-dn, up + 1)}
    n_group = max(group_of.values()) + 1
    TOTAL, DOT, FACTOR = n_group, n_group + 1, n_group + 2

    def weigh(j):
        stat[j] = jnp.max(mx[...], axis=0, keepdims=True)
        if j:
            scale = jnp.exp2((stat[j - 1] - stat[j]) * (SCALE * LOG2E))
            ot[...] = ot[...] * scale
            lr[...] = lr[...] * scale

        def one(cc, x):
            for sl in lanes:
                e = jnp.exp2((sb[cc, :, sl] - stat[j, :, sl]) * (SCALE * LOG2E))
                sb[cc, :, sl] = e
                lr[:, sl] += jnp.sum(e.reshape(T // 8, 8, 128), axis=0)
                pb[x, :, sl] = e.astype(BF16)
            ot[...] += tn(kv[cc, 1], pb[x])

        for step in [step for step, group in group_of.items() if group == j]:

            one(2 * at_z(step), 0)
            one(2 * at_z(step) + 1, 1)

    ready = {"q": False, "blocks": []}
    missing = {j: sum(8 for group in group_of.values() if group == j) for j in range(n_group)}

    def landed(step, count=1):
        missing[group_of[step]] -= count
        while missing and ready["q"] and missing[min(missing)] == 0:
            j = min(missing)
            del missing[j]
            weigh(j)

    def scores_of(cc):
        if ready["q"]:
            score(cc)
        else:
            ready["blocks"].append(cc)

    def on_own():
        load_g.wait()
        load_w.wait()
        project(t)
        scores_of(z_block("a", 0))
        landed(0, 4)

    def on_q():
        load_q.wait()
        arrive("q", q2.at[orows])
        ready["q"] = True
        for cc in ready["blocks"]:
            score(cc)
        landed(0, 0)

    def on_pair(i, j):
        pair = z_block("b", 0)
        arrive(("kv"[i], j), kv.at[pair, i, halves[j]])
        z_send("b", 1, 0, i, j)
        z_send("b", -1, 0, i, j)
        if i == 0 and j == 1:
            scores_of(pair)
        landed(0)

    def on_gx(i):
        piece = y_piece("b", 0)
        arrive(("gx", i), gb.at[piece, halves[i]])
        y_send("b", 1, 0, i)
        y_send("b", -1, 0, i)
        if i:
            project(piece)

    def on_kv(chain, way, hop, i, j):
        step = -way * hop
        if step == -up:
            step = up
        block = z_block(chain, step)
        arrive(("kv", chain, way, hop, i, j), kv.at[block, i, halves[j]])
        z_send(chain, way, hop, i, j)
        if i == 0 and j == 1:
            scores_of(block)
        landed(step)

    pieces = {}

    def piece_half(chain, step):
        step = yup if step == -yup else step
        pieces[chain, step] = pieces.get((chain, step), 0) + 1
        if pieces[chain, step] == 2:
            project(y_piece(chain, step))

    def on_g(chain, way, hop, i):
        step = yup if hop == yup else -way * hop
        here = gb.at[y_piece(chain, step), halves[i]]
        arrive(("g", chain, way, hop, i), here)
        y_send(chain, way, hop, i)
        if hop == yup:
            send(("gc", i), here, here, xdev)
        piece_half(chain, step)

    def on_gc(i):
        arrive(("gc", i), gb.at[y_piece("b", yup), halves[i]])
        piece_half("b", yup)

    us = 2.0 / 88e3
    kv_us, g_us = T * HD * 2 * us, T * DC * us
    part = functools.partial
    flows, events = {}, {}

    def flow(name, needs, delay, link, busy, wait, event):
        flows[name] = (needs, delay, link, busy, wait)
        events[name] = event

    for i in range(2):
        for j in range(2):
            flow(("kv"[i], j), (), 0, "x", kv_us / 2, 2.6, part(on_pair, i, j))
    for i in range(2):
        flow(("gx", i), (), 0, "x", g_us, 1.8, part(on_gx, i))
    flow("q", (), 0, "x", kv_us, 2.6, on_q)
    for i in range(2):
        for (chain, way), count in hops.items():
            for hop, j in [(hop, j) for hop in range(1, count + 1) for j in range(2)]:
                first = () if chain == "a" else (("kv"[i], j),)
                needs = (("kv", chain, way, hop - 1, i, j),) if hop > 1 else first
                name = ("kv", chain, way, hop, i, j)
                flow(name, needs, 0.1, ("z", way), kv_us / 2, 2.2, part(on_kv, chain, way, hop, i, j))
        for chain in "ab":
            for way in (1, -1):
                for hop in range(1, yup + 1):
                    if y_goes(chain, way, hop, i):
                        first = () if chain == "a" else (("gx", i),)
                        needs = (("g", chain, way, hop - 1, i),) if hop > 1 else first
                        late = 0.2 if i == (0 if way == -1 else 1) else 0.1
                        name = ("g", chain, way, hop, i)
                        flow(name, needs, late, ("y", way), g_us, 1.8, part(on_g, chain, way, hop, i))
                        if hop == yup:
                            flow(("gc", i), (name,), 0.1, "x", g_us, 1.8, part(on_gc, i))
    times = arrival_times(flows)

    def gather(names):
        for name in sorted(names, key=times.get):
            events[name]()

    last_g = max([times[name] for name in events if name[0] in ("g", "gx", "gc")])
    on_own()
    gather([name for name in events if times[name] <= last_g])
    ghb[0] = gh[:, :HD].astype(BF16)
    ghb[1] = gh[:, HD:].astype(BF16)
    send("do", ghb.at[o], do2.at[hrows], partner)
    do2[hrows, :] = ghb[h]
    gather([name for name in events if times[name] > last_g])

    inverse = 1.0 / jnp.sum(lr[...], axis=0, keepdims=True)
    low = (ot[...] * inverse).astype(BF16)
    ob[...] = low
    send("att", ob.at[:, orows], att.at[h], partner)
    att[h] = ob[:, hrows]
    for j in range(n_group):
        back = jnp.exp2((stat[j] - stat[n_group - 1]) * (SCALE * LOG2E))
        stat[FACTOR + j] = inverse * back
    arrive("do", do2.at[orows])
    do_t = jnp.transpose(do2[...].astype(F32))
    stat[DOT] = jnp.sum(do_t * low.astype(F32), axis=0, keepdims=True)
    dqt[...] = jnp.zeros_like(dqt)

    def gradients(step):
        zz = at_z(step)
        factor = stat.at[FACTOR + group_of[step]]

        def one(x):
            cc = 2 * zz + x
            dp = nt(kv[cc, 1], do2[...])
            for sl in lanes:
                p = sb[cc, :, sl] * factor[:, sl]
                pb[x, :, sl] = p.astype(BF16)
                db[x, :, sl] = (p * (dp[:, sl] - stat[DOT, :, sl])).astype(BF16)
            own[zz, 0, x] = SCALE * nn(db[x], q2[...])
            own[zz, 1, x] = nn(pb[x], do2[...])
            dqt[...] += tn(kv[cc, 0], db[x])

        one(0)
        one(1)

    first_hop = {(0, 1): up, (0, -1): dn, (1, 1): dn, (1, -1): up}
    slots = {1: rp, -1: rm}

    def pass_on(i, way, hop):
        zz = at_z(way * hop)
        for x in (o, h):
            total = own[zz, i, x]
            if hop < first_hop[i, way]:
                slot = slots[way].at[i, hop, x]
                arrive(("kvg", i, way, hop + 1, x is o), slot)
                total = total + slot[...].astype(F32)
            snd[zz, i, x] = total.astype(BF16)
            send(("kvg", i, way, hop, x is o), snd.at[zz, i, x], slots[way].at[i, hop - 1, x], zdev(way))

    half = ntp // 2
    per_piece = DC // CW

    def weight_part(head, part, base, out):
        piece = base * half + part
        rows = pl.ds(pl.multiple_of(head * HD, HD), HD)
        res = nn(att[head], gb[piece])
        for j in range(per_piece):
            out[part * per_piece + j, rows] = res[:, j * CW:(j + 1) * CW].astype(out.dtype)

    def weight_other(phase):
        head = o if phase else h
        rows = pl.ds(pl.multiple_of(head * HD, HD), HD)
        if phase:
            arrive("att", att.at[o])
        else:

            @pl.when(d == 0)
            def _():
                pl.semaphore_wait(here, 1)

        for part in range(half):
            weight_part(head, part, 1 - d, gws)
            block = pl.ds(part * per_piece, per_piece)
            send(("gw", phase, part), gws.at[block, rows], gwr.at[block, rows], core)

    def weight_own(phase):
        for part in range(half):
            weight_part(o if phase else h, part, d, gwo)

    def weight_cross(phase):
        head = o if phase else h
        rows = pl.ds(pl.multiple_of(head * HD, HD), HD)
        for part in range(half):
            arrive(("gw", phase, part), gwr.at[pl.ds(part * per_piece, per_piece), rows])
        for step in order:
            zz = at_z(step)
            gxs[zz, rows] = (gwo[2 * zz + o, rows] + gwr[2 * zz + o, rows].astype(F32)).astype(BF16)
            send(("gwx", phase, step), gxs.at[zz, rows], gxr.at[zz, rows], partner)

    order = [up] if nz > 1 else []
    for hop in range(dn, 0, -1):
        order += [hop, -hop]
    order += [0]
    gslots = {1: gp, -1: gm}
    tops = {1: pl.ds(0, F // 2), -1: pl.ds(F // 2, F // 2)}

    def weight_total(step):
        zz = at_z(step)
        for phase in range(2):
            head = h if phase else o
            rows = pl.ds(pl.multiple_of(head * HD, HD), HD)
            arrive(("gwx", phase, step), gxr.at[zz, rows])
        gwo[2 * zz + h] = gwo[2 * zz + h] + gwr[2 * zz + h].astype(F32) + gxr[zz].astype(F32)

    def weight_add(zz, way, hop):
        rows = tops[way] if hop == up else pl.ds(0, F)
        slot = gslots[way].at[hop - 1, rows]
        arrive(("gwz", way, hop), slot)
        gwo[2 * zz + h, rows] = gwo[2 * zz + h, rows] + slot[...].astype(F32)

    def weight_far():
        weight_total(up)
        zz = at_z(up)
        gsn[zz] = gwo[2 * zz + h].astype(BF16)
        for way in (1, -1):
            send(("gwz", way, up), gsn.at[zz, tops[way]], gslots[way].at[up - 1, tops[way]], zdev(way))

    def weight_pass(way, hop):
        weight_total(way * hop)
        zz = at_z(way * hop)
        weight_add(zz, way, hop + 1)
        gsn[zz] = gwo[2 * zz + h].astype(BF16)
        send(("gwz", way, hop), gsn.at[zz], gslots[way].at[hop - 1], zdev(way))

    def gradient_pair(hop):
        gradients(hop)
        gradients(-hop)

    def finish(i, x):
        out = (dk_hbm, dv_hbm)[i]
        total = own[z, i, x]
        for way in (1, -1):
            if first_hop[i, way] > 0:
                arrive(("kvg", i, way, 1, x is o), slots[way].at[i, 0, x])
                total = total + slots[way][i, 0, x].astype(F32)
        fin[i, x] = total.astype(BF16)
        if x is o:
            send(("fin", i), fin.at[i, o], out.at[0, :, hcols], partner)
        else:
            outs.append(local(i, fin.at[i, h], out.at[0, :, hcols]))

    outs = []

    def finish_q():
        dqb[...] = jnp.transpose(SCALE * dqt[...]).astype(BF16)
        send("dq", dqb.at[orows], dq_hbm.at[0, :, hcols], partner)
        outs.append(local(4, dqb.at[hrows], dq_hbm.at[0, :, hcols]))

    def finish_weight():
        weight_total(0)
        if nz > 1:
            weight_add(z, 1, 1)
            weight_add(z, -1, 1)
        gout[...] = gwo[2 * z + h].astype(BF16)
        outs.append(local(5, gout, gw_hbm))

    if nz > 1:
        gradients(up)
        pass_on(0, 1, up)
        pass_on(1, -1, up)
    weight_other(0)
    if dn:
        gradient_pair(dn)
        pass_on(1, 1, dn)
        pass_on(0, -1, dn)
    weight_own(0)
    work = [part(gradient_pair, hop) for hop in range(dn - 1, 0, -1)]
    work += [part(gradients, 0), finish_q]
    weight_cross(0)
    weight_other(1)
    if dn:
        pass_on(0, 1, dn)
        pass_on(1, -1, dn)
    work.pop(0)()
    weight_own(1)
    weight_cross(1)
    tasks = []
    for hop in range(dn - 1, 0, -1):
        tasks += [part(pass_on, 1, 1, hop), part(pass_on, 0, -1, hop)]
        tasks += [part(pass_on, 0, 1, hop), part(pass_on, 1, -1, hop)]
    ends = (1, 0) if dn else (0, 1)
    more = [weight_far] if nz > 1 else []
    for hop in range(dn, 0, -1):
        more += [part(weight_pass, 1, hop), part(weight_pass, -1, hop)]
    for i, task in enumerate(tasks):
        task()
        if i == 1:
            while work:
                work.pop(0)()
        if i % 2 == 1 and i >= EARLY and more:
            for task in more[:1 if more[0] is weight_far else 2]:
                task()
                more.pop(0)
    while work:
        work.pop(0)()
    for i in ends:
        finish(i, o)
    for task in more[:-2]:
        task()
    for i in ends:
        finish(i, h)
    for task in more[-2:]:
        task()
    finish_weight()

    arrive("dq", dq_hbm.at[0, :, ocols])
    arrive(("fin", 0), dk_hbm.at[0, :, ocols])
    arrive(("fin", 1), dv_hbm.at[0, :, ocols])
    for cp in outs:
        cp.wait()
    for cp in sent:
        cp.wait_send()
    assert len(sem.index) <= N_SEM


def hand_on(*refs):
    n = (len(refs) - 1) // 3
    ins, outs, bufs, sems = refs[:n], refs[n:2 * n], refs[2 * n:3 * n], refs[3 * n]
    reads = [pltpu.make_async_copy(a, b, sems.at[i]) for i, (a, b) in enumerate(zip(ins, bufs))]
    writes = [pltpu.make_async_copy(a, b, sems.at[n + i]) for i, (a, b) in enumerate(zip(bufs, outs))]
    for cp in reads:
        cp.start()
    for read, write in zip(reads, writes):
        read.wait()
        write.start()
    for cp in writes:
        cp.wait()


def per_device(nz, ny, q, k, v, g, w, pattern, offsets):
    T = q.shape[1]
    Q2 = 2 * T
    nctx, ntp = 2 * nz, 2 * ny
    DC, F = g.shape[2], w.shape[0]
    CW = w.shape[1] // (2 * nctx)
    deep = max(nz // 2, 1)
    V = pltpu.VMEM
    hbm = pl.BlockSpec(memory_space=pl.ANY)
    smem = pl.BlockSpec(memory_space=pltpu.SMEM)
    scratch = [
        V((nctx, 2, T, HD), BF16),
        V((Q2, HD), BF16),
        V((Q2, HD), BF16),
        V((ntp, T, DC), BF16),
        V(w.shape, BF16),
        V((T, F), F32),
        V((2, T, HD), BF16),
        V((nctx, T, 128), F32),
        V((nctx, 1, Q2), F32),
        V((nctx, T, Q2), F32),
        V((8, Q2), F32),
        V((8, Q2), F32),
        V((2 * deep + 4, 1, Q2), F32),
        V((HD, Q2), F32),
        V((HD, Q2), BF16),
        V((2, HD, T), BF16),
        V((2, T, Q2), BF16),
        V((2, T, Q2), BF16),
        V((nz, 2, 2, T, HD), F32),
        V((nz, 2, 2, T, HD), BF16),
        V((2, deep, 2, T, HD), BF16),
        V((2, deep, 2, T, HD), BF16),
        V((HD, Q2), F32),
        V((Q2, HD), BF16),
        V((2, 2, T, HD), BF16),
        V((nctx, F, CW), BF16),
        V((nctx, F, CW), BF16),
        V((nctx, F, CW), F32),
        V((nz, F, CW), BF16),
        V((nz, F, CW), BF16),
        V((nz, F, CW), BF16),
        V((deep, F, CW), BF16),
        V((deep, F, CW), BF16),
        V((F, CW), BF16),
        pltpu.SemaphoreType.DMA((N_SEM,)),
        pltpu.SemaphoreType.DMA((N_SEM,)),
        pltpu.SemaphoreType.DMA((6,)),
        pltpu.SemaphoreType.REGULAR,
    ]
    like = jax.ShapeDtypeStruct(q.shape, BF16)
    shapes = (like, like, like, jax.ShapeDtypeStruct((F, CW), BF16))
    results = pl.pallas_call(
        functools.partial(kernel, nz, ny),
        out_shape=shapes,
        in_specs=[smem, smem, hbm, hbm, hbm, hbm, hbm],
        out_specs=(hbm, hbm, hbm, hbm),
        scratch_shapes=scratch,
        compiler_params=pltpu.CompilerParams(
            collective_id=0, has_side_effects=True, vmem_limit_bytes=60 * 1024 * 1024
        ),
        name="attention_backward",
    )(pattern.T, offsets.T, q, k, v, g, w)
    return tuple(
        pl.pallas_call(
            hand_on,
            out_shape=shapes,
            in_specs=[hbm] * 4,
            out_specs=(hbm,) * 4,
            scratch_shapes=[V(s.shape, BF16) for s in shapes] + [pltpu.SemaphoreType.DMA((8,))],
            name="hand_on",
        )(*results)
    )


def solution(mesh):
    nz, ny = mesh.shape["ctx"] // 2, mesh.shape["tp"] // 2
    spec = P("dp", "ctx", "tp")
    return jax.shard_map(
        functools.partial(per_device, nz, ny),
        mesh=mesh,
        in_specs=(spec, spec, spec, spec, P("tp", None), P(), P()),
        out_specs=(spec, spec, spec, P("tp", ("dp", "ctx"))),
        check_vma=False,
    )
```
